32 devices in a mesh: groups: 2 (over y), tok: 16 (over z, x, core).
Axes of the slice: x: 2, y: 2, z: 4, core: 2. Of those that a mesh axis runs over, the one named last changes fastest.
Arguments:
- queries: bfloat16 [2048, 2048], P(('groups', 'tok')), parts along dimension 0, may hold values from -256 to 256, as said below
- fresh_keys: bfloat16 [2048, 2048], P(('groups', 'tok')), parts along dimension 0, may hold values from -6 to 6, as said below
- fresh_values: bfloat16 [2048, 2048], P(('groups', 'tok')), parts along dimension 0, may hold values from -6 to 6
- stale_keys: bfloat16 [2048, 2048], P(('groups', 'tok')), parts along dimension 0, may hold values from -6 to 6
- stale_values: bfloat16 [2048, 2048], P(('groups', 'tok')), parts along dimension 0, may hold values from -6 to 6
- patch_starts: int32 [32], P('groups'), parts along dimension 0, may hold values from 0 to 1023, as said below
- order_starts: int32 [32], P('groups'), parts along dimension 0, may hold values from 0 to 1023, as said below
Outputs:
- attended: bfloat16 [2048, 2048], P(('groups', 'tok')), parts along dimension 0
The draws below stay inside these ranges and needn't reach their ends.
There are 2 independent parts, one for each index of `groups`. The reference program is written for one: setup_inputs(seed, part) draws one part's arguments, and reference() takes and returns one part's arrays. A program takes and returns all parts, laid end to end along the dimension named above; each array names one. Nothing has to cross between parts.
Inputs may be any that keep to these rules, and one draw needn't show every extreme that they name: `patch_starts`: strictly increasing; the first entry is 0. `order_starts`: the entries of patch_starts, each once, in processing order. `queries`: entries are finite. `fresh_keys`: entries are finite.
All inputs are finite; a program needn't handle non-finite values.
Results may differ from the reference program's by a relative error of at most 0.0049.
Values may be sent and summed in bfloat16 or wider, within the bound.
A program may use at most 128 MiB of HBM per device.

```python
import math
import jax
import jax.numpy as jnp
from jax import lax

HEADS = 16
HEAD_DIM = 128
PATCHES = 16
TOKENS = 1024


def shared_keys(key):
    draws = jax.random.normal(jax.random.fold_in(key, 11), (TOKENS, HEADS * HEAD_DIM), jnp.float32)
    return jnp.clip(draws, -6.0, 6.0)


def draw_fresh_keys(key, part):
    return shared_keys(key).astype(jnp.bfloat16)


def draw_queries(key, part):
    base_key = jax.random.fold_in(key, 23)
    draws = jax.random.normal(base_key, (TOKENS, HEADS * HEAD_DIM), jnp.float32)
    return (3.0 * jnp.clip(draws, -4.0, 4.0)).astype(jnp.bfloat16)


def patch_layout(key):
    cut_points = jax.random.permutation(jax.random.fold_in(key, 5), TOKENS - 1)[:PATCHES - 1] + 1
    starts = jnp.concatenate([jnp.zeros((1,), jnp.int32), jnp.sort(cut_points.astype(jnp.int32))])
    ordering = jax.random.permutation(jax.random.fold_in(key, 6), PATCHES)
    return (starts, starts[ordering])


def draw_patch_starts(key, part):
    return patch_layout(key)[0].astype(jnp.int32)


def draw_order_starts(key, part):
    return patch_layout(key)[1].astype(jnp.int32)


def levels(key, extent, pieces, low, largest):
    def one(axis_at, parts):
        heights = jax.random.uniform(jax.random.fold_in(jax.random.fold_in(key, 6), axis_at), (parts,), jnp.float32, low / len(pieces), largest / len(pieces))
        return jnp.repeat(jnp.exp(heights), extent[axis_at] // parts).reshape((-1,) + (1,) * (len(extent) - axis_at - 1))

    loudness = one(*pieces[0])
    for cut in pieces[1:]:
        loudness = loudness * one(*cut)
    return loudness


def noise(rng, extent, deviation, reach, shards=(), kind=jnp.bfloat16):
    level = levels(rng, extent, shards, -0.22, 0.18) if shards else 1.0
    drawn = jax.random.normal(rng, extent, jnp.float32) * deviation * level
    return jnp.minimum(jnp.maximum(drawn, -reach), reach).astype(kind)


def setup_inputs(seed: int = 0, part: int = 0) -> dict:
    splits = jax.random.split(jax.random.key(seed), 8)
    part_keys = jax.random.split(jax.random.fold_in(splits[7], part), 8)
    queries = draw_queries(jax.random.fold_in(jax.random.fold_in(splits[7], part), 71), part)
    fresh_keys = draw_fresh_keys(jax.random.fold_in(jax.random.fold_in(splits[7], part), 71), part)
    fresh_values = noise(part_keys[2], (TOKENS, HEADS * HEAD_DIM), 1.0, 6.0, ((0, 16),))
    stale_keys = noise(part_keys[3], (TOKENS, HEADS * HEAD_DIM), 1.0, 6.0, ((0, 16),))
    stale_values = noise(part_keys[4], (TOKENS, HEADS * HEAD_DIM), 1.0, 6.0, ((0, 16),))
    patch_starts = draw_patch_starts(jax.random.fold_in(jax.random.fold_in(splits[7], part), 71), part)
    order_starts = draw_order_starts(jax.random.fold_in(jax.random.fold_in(splits[7], part), 71), part)
    return {"queries": queries, "fresh_keys": fresh_keys, "fresh_values": fresh_values, "stale_keys": stale_keys, "stale_values": stale_values, "patch_starts": patch_starts, "order_starts": order_starts}


def token_ranks(positions, patch_starts, order_starts):
    patch_count = patch_starts.shape[0]
    slot_ids = jnp.arange(patch_count, dtype=jnp.int32)
    patch_of = lax.optimization_barrier(jnp.sum((patch_starts[None, :] <= positions[:, None]).astype(jnp.int32), axis=1)) - 1
    matches = (order_starts[:, None] == patch_starts[None, :]).astype(jnp.int32)
    rank_of = lax.optimization_barrier(jnp.sum(matches * slot_ids[:, None], axis=0))
    one_hot = (patch_of[:, None] == slot_ids[None, :]).astype(jnp.int32)
    return lax.optimization_barrier(jnp.sum(one_hot * rank_of[None, :], axis=1))

def attend_block(query_block, query_rank, key_stack, key_rank):
    dims = (((1,), (1,)), ((), ()))
    score_scale = 1.0 / math.sqrt(query_block.shape[-1])
    fresh_scores = lax.dot_general(query_block, key_stack[0], dims, preferred_element_type=jnp.float32) * score_scale
    stale_scores = lax.dot_general(query_block, key_stack[2], dims, preferred_element_type=jnp.float32) * score_scale
    fresh_ok = key_rank[None, :] <= query_rank[:, None]
    fresh_scores = jnp.where(fresh_ok, fresh_scores, -jnp.inf)
    stale_scores = jnp.where(fresh_ok, -jnp.inf, stale_scores)
    row_max = jnp.maximum(lax.optimization_barrier(jnp.max(fresh_scores, axis=1)), lax.optimization_barrier(jnp.max(stale_scores, axis=1)))[:, None]
    fresh_exp = jnp.exp(fresh_scores - row_max)
    stale_exp = jnp.exp(stale_scores - row_max)
    row_total = lax.optimization_barrier(jnp.sum(fresh_exp, axis=1, keepdims=True)) + lax.optimization_barrier(jnp.sum(stale_exp, axis=1, keepdims=True))
    fresh_probs = (fresh_exp / row_total).astype(jnp.bfloat16)
    stale_probs = (stale_exp / row_total).astype(jnp.bfloat16)
    mixed = jnp.dot(fresh_probs, key_stack[1], preferred_element_type=jnp.float32)
    mixed = mixed + jnp.dot(stale_probs, key_stack[3], preferred_element_type=jnp.float32)
    return mixed.astype(jnp.bfloat16)

def attend_rows(query_rows, query_rank, key_stack, key_rank):
    row_count = query_rows.shape[0]
    block_rows = 512 if row_count % 512 == 0 else row_count
    blocks = row_count // block_rows

    def one_block(inputs):
        return attend_block(inputs[0], inputs[1], key_stack, key_rank)
    result = lax.map(one_block, (query_rows.reshape(blocks, block_rows, query_rows.shape[1]), query_rank.reshape(blocks, block_rows)))
    return result.reshape(row_count, query_rows.shape[1])

def reference(queries, fresh_keys, fresh_values, stale_keys, stale_values, patch_starts, order_starts):
    token_count = queries.shape[0]
    positions = jnp.arange(token_count, dtype=jnp.int32)
    ranks = token_ranks(positions, patch_starts, order_starts)

    def by_head(array):
        return array.reshape(token_count, HEADS, HEAD_DIM).transpose(1, 0, 2)
    stacked = jnp.stack([by_head(fresh_keys), by_head(fresh_values), by_head(stale_keys), by_head(stale_values)], axis=1)

    def one_head(inputs):
        return attend_rows(inputs[0], ranks, inputs[1], ranks)
    attended = lax.map(one_head, (by_head(queries), stacked))
    return attended.transpose(1, 0, 2).reshape(token_count, HEADS * HEAD_DIM)
```

```python
import functools
import math

import jax
import jax.numpy as jnp
from jax import lax
from jax.experimental import pallas as pl
from jax.experimental.pallas import tpu as pltpu
from jax.sharding import PartitionSpec as P

HEADS = 16
HEAD_DIM = 128
LAYER = 4
ISSUE = ((('Q', 0, False), ('K', 0, False), ('ready', 0, False), ('Q', 0, True), ('V', 0, False), ('Q', 1, False), ('pass', 0, False), ('Q', 1, True), ('K', 1, False), ('V', 1, False)), (), (('pass', 1, False),), (), (), (), ())
MESH = pl.DeviceIdType.MESH


def attention_kernel(
    devices,
    patch_starts,
    order_starts,
    queries,
    fresh_keys,
    stale_keys,
    fresh_values,
    stale_values,
    out_ref,
    q_buf,
    kv_buf,
    p_fresh,
    p_stale,
    o_buf,
    q_rank,
    k_rank,
    send_sems,
    recv_sems,
    own_sem,
    out_send,
    out_recv,
):
    me = lax.axis_index("tok")
    tok_dev = queries.shape[0]
    group_size = devices // HEADS
    slab = tok_dev // group_size
    tokens = devices * tok_dev
    rows = devices * slab
    my_head = me // group_size
    my_member = me % group_size
    barrier = pltpu.get_barrier_semaphore()

    def peer_of(step):
        return lax.rem(me + step, devices)

    def columns(head):
        return pl.ds(pl.multiple_of(head * HEAD_DIM, HEAD_DIM), HEAD_DIM)

    def row_slab(index, size):
        return pl.ds(pl.multiple_of(index * size, size), size)

    def greet(step, carry):
        pl.semaphore_signal(barrier, inc=1, device_id={"tok": peer_of(step)}, device_id_type=MESH)
        return carry

    lax.fori_loop(1, devices, greet, 0)

    sources = (queries, fresh_keys, stale_keys, fresh_values, stale_values)

    def source_view(which, device):
        head, member = device // group_size, device % group_size
        if which == 0:
            return queries.at[row_slab(member, slab), columns(head)]
        return sources[which].at[:, columns(head)]

    def landing(which, device):
        if which == 0:
            return q_buf.at[row_slab(device, slab), :]
        return kv_buf.at[which - 1, row_slab(device, tok_dev), :]

    own = [
        pltpu.make_async_copy(source_view(which, me), landing(which, me), own_sem.at[which])
        for which in range(5)
    ]
    for copy in own:
        copy.start()
    pl.semaphore_wait(barrier, devices - 1)

    for which in range(5):

        def send(step, carry, which=which):
            peer = peer_of(step)
            pltpu.make_async_remote_copy(
                src_ref=source_view(which, peer),
                dst_ref=landing(which, me),
                send_sem=send_sems.at[which],
                recv_sem=recv_sems.at[which],
                device_id={"tok": peer},
                device_id_type=MESH,
            ).start()
            return carry

        lax.fori_loop(1, devices, send, 0)

    patches = patch_starts.shape[0]
    starts = [patch_starts[p] for p in range(patches)]
    orders = [order_starts[p] for p in range(patches)]
    ranks = []
    for p in range(patches):
        rank = jnp.int32(0)
        for i in range(patches):
            rank = rank + jnp.where(orders[i] == starts[p], jnp.int32(i), jnp.int32(0))
        ranks.append(rank)
    jumps = [ranks[0]] + [ranks[p] - ranks[p - 1] for p in range(1, patches)]

    def rank_at(positions):
        total = jnp.zeros(positions.shape, jnp.int32)
        for p in range(patches):
            total = total + jnp.where(positions >= starts[p], jumps[p], 0)
        return total

    k_rank[...] = rank_at(lax.broadcasted_iota(jnp.int32, k_rank.shape, 1))

    def fill_rank(device, carry):
        base = device * tok_dev + my_member * slab
        q_rank[row_slab(device, slab), :] = rank_at(
            base + lax.broadcasted_iota(jnp.int32, (slab, HEAD_DIM), 0)
        )
        return carry

    lax.fori_loop(0, devices, fill_rank, 0)

    def all_of(which):
        size = (devices - 1) * (slab if which == 0 else tok_dev)
        return q_buf.at[0:size, :] if which == 0 else kv_buf.at[which - 1, 0:size, :]

    def arrived(which):
        view = all_of(which)
        pltpu.make_async_copy(view, view, recv_sems.at[which]).wait()
        own[which].wait()

    for which in range(3):
        arrived(which)

    score_scale = 1.0 / math.sqrt(HEAD_DIM)
    block = max(slab, min(rows, (1 << 18) // tokens))
    blocks = rows // block
    dims = (((1,), (1,)), ((), ()))

    def probs_block(i, carry):
        at = row_slab(i, block)
        q = q_buf[at, :]
        fresh = lax.dot_general(q, kv_buf[0], dims, preferred_element_type=jnp.float32)
        stale = lax.dot_general(q, kv_buf[1], dims, preferred_element_type=jnp.float32)
        fresh_ok = k_rank[0:1, :] <= q_rank[at, 0:1]
        scores = jnp.where(fresh_ok, fresh, stale) * score_scale
        top = jnp.max(scores, axis=1, keepdims=True)
        weights = jnp.exp(scores - top)
        total = jnp.sum(weights, axis=1, keepdims=True)
        probs = weights * (1.0 / total)
        p_fresh[at, :] = jnp.where(fresh_ok, probs, 0.0).astype(jnp.bfloat16)
        p_stale[at, :] = jnp.where(fresh_ok, 0.0, probs).astype(jnp.bfloat16)
        return carry

    lax.fori_loop(0, blocks, probs_block, 0)

    for which in range(3, 5):
        arrived(which)

    per_block = block // slab

    def give_back(i):
        def one(j, carry):
            target = i * per_block + j

            @pl.when(target != me)
            def _():
                pltpu.make_async_remote_copy(
                    src_ref=o_buf.at[row_slab(target, slab), :],
                    dst_ref=out_ref.at[row_slab(my_member, slab), columns(my_head)],
                    send_sem=out_send,
                    recv_sem=out_recv,
                    device_id={"tok": target},
                    device_id_type=MESH,
                ).start()

            return carry

        lax.fori_loop(0, per_block, one, 0)

    def attend_block(i, carry):
        at = row_slab(i, block)
        mixed = jnp.dot(p_fresh[at, :], kv_buf[2], preferred_element_type=jnp.float32)
        mixed = mixed + jnp.dot(p_stale[at, :], kv_buf[3], preferred_element_type=jnp.float32)
        o_buf[at, :] = mixed.astype(jnp.bfloat16)
        give_back(i)
        return carry

    lax.fori_loop(0, blocks, attend_block, 0)
    mine = pltpu.make_async_copy(
        o_buf.at[row_slab(me, slab), :],
        out_ref.at[row_slab(my_member, slab), columns(my_head)],
        own_sem.at[0],
    )
    mine.start()
    for which in range(5):
        view = all_of(which)
        pltpu.make_async_copy(view, view, send_sems.at[which]).wait()
    view = o_buf.at[0 : (devices - 1) * slab, :]
    mine.wait()
    pltpu.make_async_copy(view, view, out_send).wait()
    pltpu.make_async_copy(view, view, out_recv).wait()


def shards(queries, fresh_keys, fresh_values, stale_keys, stale_values, patch_starts, order_starts):
    devices = lax.axis_size("tok")
    tok_dev, width = queries.shape
    slab = tok_dev // (devices // HEADS)
    tokens, rows = devices * tok_dev, devices * slab
    anywhere = pl.BlockSpec(memory_space=pl.ANY)
    scalars = pl.BlockSpec(memory_space=pltpu.SMEM)
    return pl.pallas_call(
        functools.partial(attention_kernel, devices),
        out_shape=jax.ShapeDtypeStruct((tok_dev, width), jnp.bfloat16),
        in_specs=[scalars] * 2 + [anywhere] * 5,
        out_specs=anywhere,
        scratch_shapes=[
            pltpu.VMEM((rows, HEAD_DIM), jnp.bfloat16),
            pltpu.VMEM((4, tokens, HEAD_DIM), jnp.bfloat16),
            pltpu.VMEM((rows, tokens), jnp.bfloat16),
            pltpu.VMEM((rows, tokens), jnp.bfloat16),
            pltpu.VMEM((rows, HEAD_DIM), jnp.bfloat16),
            pltpu.VMEM((rows, HEAD_DIM), jnp.int32),
            pltpu.VMEM((8, tokens), jnp.int32),
            pltpu.SemaphoreType.DMA((5,)),
            pltpu.SemaphoreType.DMA((5,)),
            pltpu.SemaphoreType.DMA((5,)),
            pltpu.SemaphoreType.DMA,
            pltpu.SemaphoreType.DMA,
        ],
        compiler_params=pltpu.CompilerParams(
            collective_id=0, has_side_effects=True, vmem_limit_bytes=60 * 1024 * 1024
        ),
    )(
        patch_starts,
        order_starts,
        queries,
        fresh_keys,
        stale_keys,
        fresh_values,
        stale_values,
    )


def rank_table(patch_starts, order_starts):
    patches = patch_starts.shape[0]
    starts = [patch_starts[p] for p in range(patches)]
    orders = [order_starts[p] for p in range(patches)]
    ranks = []
    for p in range(patches):
        rank = jnp.int32(0)
        for i in range(patches):
            rank = rank + jnp.where(orders[i] == starts[p], jnp.int32(i), jnp.int32(0))
        ranks.append(rank)
    jumps = [ranks[0]] + [ranks[p] - ranks[p - 1] for p in range(1, patches)]

    def rank_at(positions):
        total = jnp.zeros(positions.shape, jnp.int32)
        for p in range(patches):
            total = total + jnp.where(positions >= starts[p], jumps[p], 0)
        return total

    return rank_at


def seat(device, half):
    shift = jnp.where(device >= half, LAYER, 0)
    return lax.rem(lax.rem(device, half) + shift, half)


def is_inner(device, half):
    return seat(device, half) >= LAYER


def halves_kernel(
    devices,
    patch_starts,
    order_starts,
    queries,
    fresh_keys,
    stale_keys,
    fresh_values,
    stale_values,
    parts_ref,
    shares_ref,
    q_buf,
    k_buf,
    v_buf,
    p_fresh,
    p_stale,
    o_buf,
    s_buf,
    stats_ref,
    shares,
    q_rank,
    k_rank,
    q_send,
    q_recv,
    k_send,
    k_recv,
    v_send,
    v_recv,
    own_sem,
    o_send,
    o_recv,
    s_send,
    s_recv,
    ready,
    lse,
    twin_lse,
    twin_part,
    edge_part,
    pass_send,
    l_send,
    l_recv,
    t_send,
    t_recv,
):
    me = lax.axis_index("tok")
    tok_dev = queries.shape[0]
    half = devices // 2
    held = HEADS // half
    tokens = devices * tok_dev
    keys = half * tok_dev
    side, place = lax.div(me, half), lax.rem(me, half)
    outer_rows = LAYER * tok_dev
    my_group = seat(me, half)
    inner = my_group >= LAYER
    outer = jnp.logical_not(inner)
    outward = jnp.where(side == 0, -LAYER, LAYER)
    twin = me - outward
    near_outer = jnp.where(side == 0, 0, devices - LAYER)
    far_outer = devices - LAYER - near_outer
    barrier = pltpu.get_barrier_semaphore()

    def near_peer(step):
        return side * half + lax.rem(place + step, half)

    def far_peer(step):
        return (1 - side) * half + lax.rem(place + step, half)

    def columns(head):
        return pl.ds(pl.multiple_of(head * HEAD_DIM, HEAD_DIM), HEAD_DIM)

    def row_slab(index, size, count=1):
        return pl.ds(pl.multiple_of(index * size, size), size * count)

    def signal(sem, device):
        pl.semaphore_signal(sem, inc=1, device_id={"tok": device}, device_id_type=MESH)

    def greet(step, carry):
        signal(barrier, near_peer(step))
        return carry

    @pl.when(inner)
    def _():
        signal(barrier, twin)

    lax.fori_loop(1, half, greet, 0)

    def send(src, dst, send_sem, recv_sem, device):
        pltpu.make_async_remote_copy(
            src_ref=src,
            dst_ref=dst,
            send_sem=send_sem,
            recv_sem=recv_sem,
            device_id={"tok": device},
            device_id_type=MESH,
        ).start()

    sources = {"Q": (queries,), "K": (fresh_keys, stale_keys), "V": (fresh_values, stale_values)}
    near_sems = {"Q": (q_send, q_recv), "K": (k_send, k_recv), "V": (v_send, v_recv)}

    def landing(kind, head, which):
        if kind == "Q":
            return q_buf.at[head, row_slab(me, tok_dev), :]
        return (k_buf if kind == "K" else v_buf).at[head, which, row_slab(place, tok_dev), :]

    def source(kind, head, which, device):
        return sources[kind][which].at[:, columns(seat(device, half) * held + head)]

    def share_out(kind, head, far=False):
        def one(step, carry):
            peer = far_peer(step) if far else near_peer(step)
            for which in range(len(sources[kind])):
                at = (head, which)
                recv_at = at
                if kind == "Q" and not far:
                    passed_on = jnp.logical_and(outer, is_inner(peer, half))
                    recv_at = (head, passed_on.astype(jnp.int32))

                def go(which=which, at=at, recv_at=recv_at, peer=peer):
                    send(
                        source(kind, head, which, peer),
                        landing(kind, head, which),
                        near_sems[kind][0].at[at],
                        near_sems[kind][1].at[recv_at],
                        peer,
                    )

                if far:
                    pl.when(jnp.logical_or(inner, jnp.logical_not(is_inner(peer, half))))(go)
                else:
                    go()
            return carry

        lax.fori_loop(0 if far else 1, half, one, 0)

    def pass_on(head):
        @pl.when(inner)
        def _():
            view = q_buf.at[head, row_slab(near_outer, tok_dev, LAYER), :]
            pltpu.make_async_copy(view, view, q_recv.at[head, 1]).wait()
            send(view, view, pass_send.at[head], q_recv.at[head, 0], twin)

    def start_all(steps):
        for kind, head, far in steps:
            if kind == "pass":
                pass_on(head)
            elif kind == "ready":
                pl.semaphore_wait(ready, 1)

                @pl.when(inner)
                def _():
                    signal(ready, me + outward)

            else:
                share_out(kind, head, far)

    pl.semaphore_wait(barrier, half - 1 + inner.astype(jnp.int32))

    @pl.when(inner)
    def _():
        signal(ready, twin)

    start_all(ISSUE[0])

    own = {}
    for n, (kind, head, which) in enumerate(
        (kind, head, which)
        for head in range(held)
        for kind in "QKV"
        for which in range(len(sources[kind]))
    ):
        own[kind, head, which] = pltpu.make_async_copy(
            source(kind, head, which, me), landing(kind, head, which), own_sem.at[n]
        )
        own[kind, head, which].start()

    rank_at = rank_table(patch_starts, order_starts)
    k_rank[...] = rank_at(keys * side + lax.broadcasted_iota(jnp.int32, k_rank.shape, 1))

    def fill_rank(device, carry):
        q_rank[row_slab(device, tok_dev), :] = rank_at(
            device * tok_dev + lax.broadcasted_iota(jnp.int32, (tok_dev, HEAD_DIM), 0)
        )
        return carry

    lax.fori_loop(0, devices, fill_rank, 0)

    def whole_wait(view, sem):
        pltpu.make_async_copy(view, view, sem).wait()

    def slabs_of(head, count):
        return q_buf.at[head, 0 : count * tok_dev, :]

    def all_of(kind, head, which):
        return (k_buf if kind == "K" else v_buf).at[head, which, 0 : (half - 1) * tok_dev, :]

    def arrived(kind, head):
        for which in range(len(sources[kind])):
            if kind == "Q":
                arriving = devices - 1

                @pl.when(inner)
                def _():
                    whole_wait(slabs_of(head, arriving - LAYER), q_recv.at[head, 0])

                @pl.when(outer)
                def _():
                    whole_wait(slabs_of(head, arriving), q_recv.at[head, 0])

            else:
                whole_wait(all_of(kind, head, which), near_sems[kind][1].at[head, which])
            own[kind, head, which].wait()

    score_scale = 1.0 / math.sqrt(HEAD_DIM)
    block = min(tokens, 512)
    blocks = tokens // block
    per_block = block // tok_dev
    dims = (((1,), (1,)), ((), ()))
    owner_tile = 128 // tok_dev
    edge_tiles = outer_rows // 128

    def hand_out(head, target):
        send(
            o_buf.at[head, row_slab(target, tok_dev), :],
            parts_ref.at[side, :, columns(my_group * held + head)],
            o_send.at[head],
            o_recv.at[head],
            target,
        )

    def join(head):
        @pl.when(inner)
        def _():
            whole_wait(twin_lse.at[head], l_recv.at[head])
            whole_wait(twin_part.at[head], t_recv.at[head])
            for tile in range(edge_tiles):
                mine, theirs = lse[head, near_outer // owner_tile + tile], twin_lse[head, tile]
                w_mine = jnp.broadcast_to(1.0 / (1.0 + jnp.exp(theirs - mine)), (128, 128))
                w_theirs = jnp.broadcast_to(1.0 / (1.0 + jnp.exp(mine - theirs)), (128, 128))
                spot = slice(tile * 128, (tile + 1) * 128)
                full = edge_part[head, spot, :] * jnp.transpose(w_mine)
                full = full + twin_part[head, spot, :].astype(jnp.float32) * jnp.transpose(w_theirs)
                at = pl.ds(pl.multiple_of(near_outer * tok_dev + tile * 128, 128), 128)
                o_buf[head, at, :] = full.astype(jnp.bfloat16)

            def one(j, carry):
                hand_out(head, near_outer + j)
                return carry

            lax.fori_loop(0, LAYER, one, 0)


    for head in range(held):
        arrived("K", head)
        arrived("Q", head)
        start_all(ISSUE[1 + 3 * head])

        def probs_block(i, carry, head=head):
            at = row_slab(i, block)
            q = q_buf[head, at, :]
            fresh = lax.dot_general(q, k_buf[head, 0], dims, preferred_element_type=jnp.float32)
            stale = lax.dot_general(q, k_buf[head, 1], dims, preferred_element_type=jnp.float32)
            fresh_ok = k_rank[0:1, :] <= q_rank[at, 0:1]
            scores = jnp.where(fresh_ok, fresh, stale) * score_scale
            top = jnp.max(scores, axis=1, keepdims=True)
            weights = jnp.exp(scores - top)
            total = jnp.sum(weights, axis=1, keepdims=True)
            probs = weights * (1.0 / total)
            p_fresh[head, at, :] = jnp.where(fresh_ok, probs, 0.0).astype(jnp.bfloat16)
            p_stale[head, at, :] = jnp.where(fresh_ok, 0.0, probs).astype(jnp.bfloat16)
            level = jnp.broadcast_to(top + jnp.log(total), (block, 128))
            for tile in range(block // 128):
                turned = jnp.transpose(level[tile * 128 : (tile + 1) * 128, :])
                s_buf[i * (block // 128) + tile, head : head + 1, :] = turned[0:1, :]
                lse[head, i * (block // 128) + tile] = turned[0:1, :]
            return carry

        lax.fori_loop(0, blocks, probs_block, 0)
        start_all(ISSUE[2 + 3 * head])

        @pl.when(inner)
        def _(head=head):
            src = lse.at[head, pl.ds(far_outer // owner_tile, edge_tiles)]
            send(src, twin_lse.at[head], l_send.at[head], l_recv.at[head], twin)

        if head > 0:
            join(head - 1)

        if head == held - 1:

            def send_stats(step, carry):
                peer = lax.rem(me + step, devices)
                send(s_buf.at[lax.div(peer, owner_tile)], stats_ref.at[me], s_send, s_recv, peer)
                return carry

            lax.fori_loop(1, devices, send_stats, 0)

        arrived("V", head)
        start_all(ISSUE[3 + 3 * head])

        def attend_block(n, carry, head=head):
            i = lax.rem(n + (1 - side) * (blocks // 2), blocks)
            at = row_slab(i, block)
            mixed = jnp.dot(p_fresh[head, at, :], v_buf[head, 0], preferred_element_type=jnp.float32)
            mixed = mixed + jnp.dot(
                p_stale[head, at, :], v_buf[head, 1], preferred_element_type=jnp.float32
            )
            o_buf[head, at, :] = mixed.astype(jnp.bfloat16)
            near = i == side

            @pl.when(jnp.logical_and(inner, near))
            def _():
                begin = jnp.where(side == 0, 0, block - outer_rows)
                for first in (0, block - outer_rows):

                    @pl.when(begin == first)
                    def _(first=first):
                        edge_part[head] = mixed[first : first + outer_rows, :]

            @pl.when(jnp.logical_and(inner, jnp.logical_not(near)))
            def _():
                src = o_buf.at[head, row_slab(far_outer, tok_dev, LAYER), :]
                send(src, twin_part.at[head], t_send.at[head], t_recv.at[head], twin)

            def give_back(j, carry):
                target = i * per_block + j
                direct = jnp.logical_or(outer, is_inner(target, half))

                @pl.when(jnp.logical_and(target != me, direct))
                def _():
                    hand_out(head, target)

                return carry

            lax.fori_loop(0, per_block, give_back, 0)
            return carry

        lax.fori_loop(0, blocks, attend_block, 0)

    join(held - 1)
    mine = [
        pltpu.make_async_copy(
            o_buf.at[head, row_slab(me, tok_dev), :],
            parts_ref.at[side, :, columns(my_group * held + head)],
            own_sem.at[1 + head],
        )
        for head in range(held)
    ]
    mine.append(
        pltpu.make_async_copy(
            s_buf.at[lax.div(me, owner_tile)], stats_ref.at[me], own_sem.at[1 + held]
        )
    )
    for copy in mine:
        copy.start()
    s_all = stats_ref.at[0 : devices - 1]
    whole_wait(s_all, s_recv)
    mine[-1].wait()

    def levels(of_side):
        return jnp.concatenate(
            [
                stats_ref[
                    of_side * half + (head // held + of_side * LAYER) % half,
                    head % held : head % held + 1,
                    :,
                ]
                for head in range(HEADS)
            ],
            axis=0,
        )

    low, high = levels(0), levels(1)
    joined = lax.broadcasted_iota(jnp.int32, low.shape, 0) >= LAYER * held
    joined = jnp.logical_and(joined, outer)
    on_low = (side == 0).astype(jnp.float32)
    share = jnp.concatenate(
        [
            jnp.where(joined, on_low, 1.0 / (1.0 + jnp.exp(high - low))),
            jnp.where(joined, 1.0 - on_low, 1.0 / (1.0 + jnp.exp(low - high))),
            jnp.zeros((128 - 2 * HEADS, 128), jnp.float32),
        ],
        axis=0,
    )
    shares[...] = jnp.transpose(share)
    put_shares = pltpu.make_async_copy(
        shares.at[row_slab(lax.rem(me, owner_tile), tok_dev), :], shares_ref, own_sem.at[0]
    )
    put_shares.start()
    for head in range(held):
        for kind in "KV":
            for which in range(2):
                whole_wait(all_of(kind, head, which), near_sems[kind][0].at[head, which])

        @pl.when(inner)
        def _(head=head):
            whole_wait(slabs_of(head, devices - 1), q_send.at[head, 0])
            whole_wait(slabs_of(head, LAYER), pass_send.at[head])
            whole_wait(twin_lse.at[head], l_send.at[head])
            whole_wait(twin_part.at[head], t_send.at[head])

        @pl.when(outer)
        def _(head=head):
            whole_wait(slabs_of(head, devices - 1 - LAYER), q_send.at[head, 0])

    for copy in mine[:-1]:
        copy.wait()
    whole_wait(s_all, s_send)
    for head in range(held):
        most = o_buf.at[head, 0 : (devices - 1) * tok_dev, :]
        less = o_buf.at[head, 0 : (devices - 1 - LAYER) * tok_dev, :]

        @pl.when(inner)
        def _(head=head, most=most, less=less):
            whole_wait(less, o_send.at[head])
            whole_wait(most, o_recv.at[head])

        @pl.when(outer)
        def _(head=head, most=most, less=less):
            whole_wait(most, o_send.at[head])
            whole_wait(less, o_recv.at[head])

    put_shares.wait()


def merge_kernel(devices, parts_in, shares_in, out_ref, parts, mine, merged, sems, out_sems):
    me = lax.axis_index("tok")
    half = devices // 2
    outer = jnp.logical_not(is_inner(me, half))
    side = lax.div(me, half)
    direct = LAYER * (HEADS // half)
    width = out_ref.shape[1]
    chunks = out_sems.shape[0]
    wide = width // chunks
    spans = [pl.ds(chunk * wide, wide) for chunk in range(chunks)]
    shares_copy = pltpu.make_async_copy(shares_in, mine, sems.at[chunks])
    shares_copy.start()
    copies = [
        pltpu.make_async_copy(parts_in.at[:, :, at], parts.at[:, :, at], sems.at[chunk])
        for chunk, at in enumerate(spans)
    ]
    for copy in copies:
        copy.start()
    shares_copy.wait()
    outs = []
    for chunk, span in enumerate(spans):
        copies[chunk].wait()
        for head in range(chunk * wide // HEAD_DIM, (chunk + 1) * wide // HEAD_DIM):
            at = slice(head * HEAD_DIM, (head + 1) * HEAD_DIM)

            def both(at=at, head=head):
                low = parts[0, :, at].astype(jnp.float32) * mine[:, head : head + 1]
                high = parts[1, :, at].astype(jnp.float32) * mine[:, HEADS + head : HEADS + head + 1]
                merged[:, at] = (low + high).astype(jnp.bfloat16)

            if head < direct:
                both()
            else:
                pl.when(jnp.logical_not(outer))(both)

                @pl.when(outer)
                def _(at=at):
                    merged[:, at] = parts[side, :, at]

        out = pltpu.make_async_copy(merged.at[:, span], out_ref.at[:, span], out_sems.at[chunk])
        out.start()
        outs.append(out)
    for out in outs:
        out.wait()


def halves(queries, fresh_keys, fresh_values, stale_keys, stale_values, patch_starts, order_starts):
    devices = lax.axis_size("tok")
    tok_dev, width = queries.shape
    half = devices // 2
    held = HEADS // half
    tokens, keys = devices * tok_dev, half * tok_dev
    anywhere = pl.BlockSpec(memory_space=pl.ANY)
    scalars = pl.BlockSpec(memory_space=pltpu.SMEM)
    dma = pltpu.SemaphoreType.DMA
    parts, shares = pl.pallas_call(
        functools.partial(halves_kernel, devices),
        out_shape=(
            jax.ShapeDtypeStruct((2, tok_dev, width), jnp.bfloat16),
            jax.ShapeDtypeStruct((tok_dev, 128), jnp.float32),
        ),
        in_specs=[scalars] * 2 + [anywhere] * 5,
        out_specs=(anywhere, anywhere),
        scratch_shapes=[
            pltpu.VMEM((held, tokens, HEAD_DIM), jnp.bfloat16),
            pltpu.VMEM((held, 2, keys, HEAD_DIM), jnp.bfloat16),
            pltpu.VMEM((held, 2, keys, HEAD_DIM), jnp.bfloat16),
            pltpu.VMEM((held, tokens, keys), jnp.bfloat16),
            pltpu.VMEM((held, tokens, keys), jnp.bfloat16),
            pltpu.VMEM((held, tokens, HEAD_DIM), jnp.bfloat16),
            pltpu.VMEM((tokens // 128, held, 128), jnp.float32),
            pltpu.VMEM((devices, held, 128), jnp.float32),
            pltpu.VMEM((128, 128), jnp.float32),
            pltpu.VMEM((tokens, HEAD_DIM), jnp.int32),
            pltpu.VMEM((8, keys), jnp.int32),
            dma((held, 1)),
            dma((held, 2)),
            dma((held, 2)),
            dma((held, 2)),
            dma((held, 2)),
            dma((held, 2)),
            dma((5 * held,)),
            dma((held,)),
            dma((held,)),
            dma,
            dma,
            pltpu.SemaphoreType.REGULAR,
            pltpu.VMEM((held, tokens // 128, 1, 128), jnp.float32),
            pltpu.VMEM((held, LAYER * tok_dev // 128, 1, 128), jnp.float32),
            pltpu.VMEM((held, LAYER * tok_dev, HEAD_DIM), jnp.bfloat16),
            pltpu.VMEM((held, LAYER * tok_dev, HEAD_DIM), jnp.float32),
            dma((held,)),
            dma((held,)),
            dma((held,)),
            dma((held,)),
            dma((held,)),
        ],
        compiler_params=pltpu.CompilerParams(
            collective_id=0, has_side_effects=True, vmem_limit_bytes=60 * 1024 * 1024
        ),
    )(patch_starts, order_starts, queries, fresh_keys, stale_keys, fresh_values, stale_values)
    return pl.pallas_call(
        functools.partial(merge_kernel, devices),
        out_shape=jax.ShapeDtypeStruct((tok_dev, width), jnp.bfloat16),
        in_specs=[anywhere, anywhere],
        out_specs=anywhere,
        scratch_shapes=[
            pltpu.VMEM((2, tok_dev, width), jnp.bfloat16),
            pltpu.VMEM((tok_dev, 128), jnp.float32),
            pltpu.VMEM((tok_dev, width), jnp.bfloat16),
            dma((3,)),
            dma((2,)),
        ],
        compiler_params=pltpu.CompilerParams(vmem_limit_bytes=60 * 1024 * 1024),
    )(parts, shares)


def solution(mesh):
    placed = (P(("groups", "tok"), None),) * 5 + (P("groups"),) * 2
    devices = mesh.shape["tok"]

    def body(*arrays):
        tok_dev = arrays[0].shape[0]
        split = devices % 2 == 0 and HEADS % (devices // 2) == 0
        split = split and devices // 2 == 2 * LAYER and LAYER * tok_dev % 128 == 0
        split = split and 2 * LAYER * tok_dev == 512
        split = split and 128 % tok_dev == 0 and devices * tok_dev % 512 == 0
        return (halves if split else shards)(*arrays)

    return jax.shard_map(
        body, mesh=mesh, in_specs=placed, out_specs=P(("groups", "tok"), None), check_vma=False
    )
```

```python
import functools
import math

import jax
import jax.numpy as jnp
from jax import lax
from jax.experimental import pallas as pl
from jax.experimental.pallas import tpu as pltpu
from jax.sharding import PartitionSpec as P

HEADS = 16
HEAD_DIM = 128
LAYER = 4
ISSUE = ((('Q', 0, False), ('K', 0, False), ('ready', 0, False), ('Q', 0, True), ('V', 0, False), ('Q', 1, False), ('pass', 0, False), ('Q', 1, True), ('K', 1, False), ('V', 1, False)), (), (('pass', 1, False),), (), (), (), ())
MESH = pl.DeviceIdType.MESH


def attention_kernel(
    devices,
    patch_starts,
    order_starts,
    queries,
    fresh_keys,
    stale_keys,
    fresh_values,
    stale_values,
    out_ref,
    q_buf,
    kv_buf,
    p_fresh,
    p_stale,
    o_buf,
    q_rank,
    k_rank,
    send_sems,
    recv_sems,
    own_sem,
    out_send,
    out_recv,
):
    me = lax.axis_index("tok")
    tok_dev = queries.shape[0]
    group_size = devices // HEADS
    slab = tok_dev // group_size
    tokens = devices * tok_dev
    rows = devices * slab
    my_head = me // group_size
    my_member = me % group_size
    barrier = pltpu.get_barrier_semaphore()

    def peer_of(step):
        return lax.rem(me + step, devices)

    def columns(head):
        return pl.ds(pl.multiple_of(head * HEAD_DIM, HEAD_DIM), HEAD_DIM)

    def row_slab(index, size):
        return pl.ds(pl.multiple_of(index * size, size), size)

    def greet(step, carry):
        pl.semaphore_signal(barrier, inc=1, device_id={"tok": peer_of(step)}, device_id_type=MESH)
        return carry

    lax.fori_loop(1, devices, greet, 0)

    sources = (queries, fresh_keys, stale_keys, fresh_values, stale_values)

    def source_view(which, device):
        head, member = device // group_size, device % group_size
        if which == 0:
            return queries.at[row_slab(member, slab), columns(head)]
        return sources[which].at[:, columns(head)]

    def landing(which, device):
        if which == 0:
            return q_buf.at[row_slab(device, slab), :]
        return kv_buf.at[which - 1, row_slab(device, tok_dev), :]

    own = [
        pltpu.make_async_copy(source_view(which, me), landing(which, me), own_sem.at[which])
        for which in range(5)
    ]
    for copy in own:
        copy.start()
    pl.semaphore_wait(barrier, devices - 1)

    for which in range(5):

        def send(step, carry, which=which):
            peer = peer_of(step)
            pltpu.make_async_remote_copy(
                src_ref=source_view(which, peer),
                dst_ref=landing(which, me),
                send_sem=send_sems.at[which],
                recv_sem=recv_sems.at[which],
                device_id={"tok": peer},
                device_id_type=MESH,
            ).start()
            return carry

        lax.fori_loop(1, devices, send, 0)

    patches = patch_starts.shape[0]
    starts = [patch_starts[p] for p in range(patches)]
    orders = [order_starts[p] for p in range(patches)]
    ranks = []
    for p in range(patches):
        rank = jnp.int32(0)
        for i in range(patches):
            rank = rank + jnp.where(orders[i] == starts[p], jnp.int32(i), jnp.int32(0))
        ranks.append(rank)
    jumps = [ranks[0]] + [ranks[p] - ranks[p - 1] for p in range(1, patches)]

    def rank_at(positions):
        total = jnp.zeros(positions.shape, jnp.int32)
        for p in range(patches):
            total = total + jnp.where(positions >= starts[p], jumps[p], 0)
        return total

    k_rank[...] = rank_at(lax.broadcasted_iota(jnp.int32, k_rank.shape, 1))

    def fill_rank(device, carry):
        base = device * tok_dev + my_member * slab
        q_rank[row_slab(device, slab), :] = rank_at(
            base + lax.broadcasted_iota(jnp.int32, (slab, HEAD_DIM), 0)
        )
        return carry

    lax.fori_loop(0, devices, fill_rank, 0)

    def all_of(which):
        size = (devices - 1) * (slab if which == 0 else tok_dev)
        return q_buf.at[0:size, :] if which == 0 else kv_buf.at[which - 1, 0:size, :]

    def arrived(which):
        view = all_of(which)
        pltpu.make_async_copy(view, view, recv_sems.at[which]).wait()
        own[which].wait()

    for which in range(3):
        arrived(which)

    score_scale = 1.0 / math.sqrt(HEAD_DIM)
    block = max(slab, min(rows, (1 << 18) // tokens))
    blocks = rows // block
    dims = (((1,), (1,)), ((), ()))

    def probs_block(i, carry):
        at = row_slab(i, block)
        q = q_buf[at, :]
        fresh = lax.dot_general(q, kv_buf[0], dims, preferred_element_type=jnp.float32)
        stale = lax.dot_general(q, kv_buf[1], dims, preferred_element_type=jnp.float32)
        fresh_ok = k_rank[0:1, :] <= q_rank[at, 0:1]
        scores = jnp.where(fresh_ok, fresh, stale) * score_scale
        top = jnp.max(scores, axis=1, keepdims=True)
        weights = jnp.exp(scores - top)
        total = jnp.sum(weights, axis=1, keepdims=True)
        probs = weights * (1.0 / total)
        p_fresh[at, :] = jnp.where(fresh_ok, probs, 0.0).astype(jnp.bfloat16)
        p_stale[at, :] = jnp.where(fresh_ok, 0.0, probs).astype(jnp.bfloat16)
        return carry

    lax.fori_loop(0, blocks, probs_block, 0)

    for which in range(3, 5):
        arrived(which)

    per_block = block // slab

    def give_back(i):
        def one(j, carry):
            target = i * per_block + j

            @pl.when(target != me)
            def _():
                pltpu.make_async_remote_copy(
                    src_ref=o_buf.at[row_slab(target, slab), :],
                    dst_ref=out_ref.at[row_slab(my_member, slab), columns(my_head)],
                    send_sem=out_send,
                    recv_sem=out_recv,
                    device_id={"tok": target},
                    device_id_type=MESH,
                ).start()

            return carry

        lax.fori_loop(0, per_block, one, 0)

    def attend_block(i, carry):
        at = row_slab(i, block)
        mixed = jnp.dot(p_fresh[at, :], kv_buf[2], preferred_element_type=jnp.float32)
        mixed = mixed + jnp.dot(p_stale[at, :], kv_buf[3], preferred_element_type=jnp.float32)
        o_buf[at, :] = mixed.astype(jnp.bfloat16)
        give_back(i)
        return carry

    lax.fori_loop(0, blocks, attend_block, 0)
    mine = pltpu.make_async_copy(
        o_buf.at[row_slab(me, slab), :],
        out_ref.at[row_slab(my_member, slab), columns(my_head)],
        own_sem.at[0],
    )
    mine.start()
    for which in range(5):
        view = all_of(which)
        pltpu.make_async_copy(view, view, send_sems.at[which]).wait()
    view = o_buf.at[0 : (devices - 1) * slab, :]
    mine.wait()
    pltpu.make_async_copy(view, view, out_send).wait()
    pltpu.make_async_copy(view, view, out_recv).wait()


def shards(queries, fresh_keys, fresh_values, stale_keys, stale_values, patch_starts, order_starts):
    devices = lax.axis_size("tok")
    tok_dev, width = queries.shape
    slab = tok_dev // (devices // HEADS)
    tokens, rows = devices * tok_dev, devices * slab
    anywhere = pl.BlockSpec(memory_space=pl.ANY)
    scalars = pl.BlockSpec(memory_space=pltpu.SMEM)
    return pl.pallas_call(
        functools.partial(attention_kernel, devices),
        out_shape=jax.ShapeDtypeStruct((tok_dev, width), jnp.bfloat16),
        in_specs=[scalars] * 2 + [anywhere] * 5,
        out_specs=anywhere,
        scratch_shapes=[
            pltpu.VMEM((rows, HEAD_DIM), jnp.bfloat16),
            pltpu.VMEM((4, tokens, HEAD_DIM), jnp.bfloat16),
            pltpu.VMEM((rows, tokens), jnp.bfloat16),
            pltpu.VMEM((rows, tokens), jnp.bfloat16),
            pltpu.VMEM((rows, HEAD_DIM), jnp.bfloat16),
            pltpu.VMEM((rows, HEAD_DIM), jnp.int32),
            pltpu.VMEM((8, tokens), jnp.int32),
            pltpu.SemaphoreType.DMA((5,)),
            pltpu.SemaphoreType.DMA((5,)),
            pltpu.SemaphoreType.DMA((5,)),
            pltpu.SemaphoreType.DMA,
            pltpu.SemaphoreType.DMA,
        ],
        compiler_params=pltpu.CompilerParams(
            collective_id=0, has_side_effects=True, vmem_limit_bytes=60 * 1024 * 1024
        ),
    )(
        patch_starts,
        order_starts,
        queries,
        fresh_keys,
        stale_keys,
        fresh_values,
        stale_values,
    )


def rank_table(patch_starts, order_starts):
    patches = patch_starts.shape[0]
    starts = [patch_starts[p] for p in range(patches)]
    orders = [order_starts[p] for p in range(patches)]
    ranks = []
    for p in range(patches):
        rank = jnp.int32(0)
        for i in range(patches):
            rank = rank + jnp.where(orders[i] == starts[p], jnp.int32(i), jnp.int32(0))
        ranks.append(rank)
    jumps = [ranks[0]] + [ranks[p] - ranks[p - 1] for p in range(1, patches)]

    def rank_at(positions):
        total = jnp.zeros(positions.shape, jnp.int32)
        for p in range(patches):
            total = total + jnp.where(positions >= starts[p], jumps[p], 0)
        return total

    return rank_at


def seat(device, half):
    shift = jnp.where(device >= half, LAYER, 0)
    return lax.rem(lax.rem(device, half) + shift, half)


def is_inner(device, half):
    return seat(device, half) >= LAYER


def halves_kernel(
    devices,
    starts_in,
    orders_in,
    queries,
    fresh_keys,
    stale_keys,
    fresh_values,
    stale_values,
    parts_ref,
    shares_ref,
    q_buf,
    k_buf,
    v_buf,
    p_fresh,
    p_stale,
    o_buf,
    s_buf,
    stats_ref,
    shares,
    q_rank,
    k_rank,
    q_send,
    q_recv,
    k_send,
    k_recv,
    v_send,
    v_recv,
    own_sem,
    o_send,
    o_recv,
    s_send,
    s_recv,
    ready,
    layout,
    layout_sem,
    lse,
    twin_lse,
    twin_part,
    edge_part,
    pass_send,
    l_send,
    l_recv,
    t_send,
    t_recv,
):
    me = lax.axis_index("tok")
    tok_dev = queries.shape[0]
    half = devices // 2
    held = HEADS // half
    tokens = devices * tok_dev
    keys = half * tok_dev
    side, place = lax.div(me, half), lax.rem(me, half)
    outer_rows = LAYER * tok_dev
    my_group = seat(me, half)
    inner = my_group >= LAYER
    outer = jnp.logical_not(inner)
    outward = jnp.where(side == 0, -LAYER, LAYER)
    twin = me - outward
    near_outer = jnp.where(side == 0, 0, devices - LAYER)
    far_outer = devices - LAYER - near_outer
    barrier = pltpu.get_barrier_semaphore()

    def near_peer(step):
        return side * half + lax.rem(place + step, half)

    def far_peer(step):
        return (1 - side) * half + lax.rem(place + step, half)

    def columns(head):
        return pl.ds(pl.multiple_of(head * HEAD_DIM, HEAD_DIM), HEAD_DIM)

    def row_slab(index, size, count=1):
        return pl.ds(pl.multiple_of(index * size, size), size * count)

    def signal(sem, device):
        pl.semaphore_signal(sem, inc=1, device_id={"tok": device}, device_id_type=MESH)

    def greet(step, carry):
        signal(barrier, near_peer(step))
        return carry

    @pl.when(inner)
    def _():
        signal(barrier, twin)

    lax.fori_loop(1, half, greet, 0)
    layout_copies = [
        pltpu.make_async_copy(whole, layout.at[n], layout_sem.at[n])
        for n, whole in enumerate((starts_in, orders_in))
    ]
    for copy in layout_copies:
        copy.start()

    def send(src, dst, send_sem, recv_sem, device):
        pltpu.make_async_remote_copy(
            src_ref=src,
            dst_ref=dst,
            send_sem=send_sem,
            recv_sem=recv_sem,
            device_id={"tok": device},
            device_id_type=MESH,
        ).start()

    sources = {"Q": (queries,), "K": (fresh_keys, stale_keys), "V": (fresh_values, stale_values)}
    near_sems = {"Q": (q_send, q_recv), "K": (k_send, k_recv), "V": (v_send, v_recv)}

    def landing(kind, head, which):
        if kind == "Q":
            return q_buf.at[head, row_slab(me, tok_dev), :]
        return (k_buf if kind == "K" else v_buf).at[head, which, row_slab(place, tok_dev), :]

    def source(kind, head, which, device):
        return sources[kind][which].at[:, columns(seat(device, half) * held + head)]

    def share_out(kind, head, far=False):
        def one(step, carry):
            peer = far_peer(step) if far else near_peer(step)
            for which in range(len(sources[kind])):
                at = (head, which)
                recv_at = at
                if kind == "Q" and not far:
                    passed_on = jnp.logical_and(outer, is_inner(peer, half))
                    recv_at = (head, passed_on.astype(jnp.int32))

                def go(which=which, at=at, recv_at=recv_at, peer=peer):
                    send(
                        source(kind, head, which, peer),
                        landing(kind, head, which),
                        near_sems[kind][0].at[at],
                        near_sems[kind][1].at[recv_at],
                        peer,
                    )

                if far:
                    pl.when(jnp.logical_or(inner, jnp.logical_not(is_inner(peer, half))))(go)
                else:
                    go()
            return carry

        lax.fori_loop(0 if far else 1, half, one, 0)

    def pass_on(head):
        @pl.when(inner)
        def _():
            view = q_buf.at[head, row_slab(near_outer, tok_dev, LAYER), :]
            pltpu.make_async_copy(view, view, q_recv.at[head, 1]).wait()
            send(view, view, pass_send.at[head], q_recv.at[head, 0], twin)

    def start_all(steps):
        for kind, head, far in steps:
            if kind == "pass":
                pass_on(head)
            elif kind == "ready":
                pl.semaphore_wait(ready, 1)

                @pl.when(inner)
                def _():
                    signal(ready, me + outward)

            else:
                share_out(kind, head, far)

    pl.semaphore_wait(barrier, half - 1 + inner.astype(jnp.int32))

    @pl.when(inner)
    def _():
        signal(ready, twin)

    start_all(ISSUE[0])

    own = {}
    for n, (kind, head, which) in enumerate(
        (kind, head, which)
        for head in range(held)
        for kind in "QKV"
        for which in range(len(sources[kind]))
    ):
        own[kind, head, which] = pltpu.make_async_copy(
            source(kind, head, which, me), landing(kind, head, which), own_sem.at[n]
        )
        own[kind, head, which].start()

    for copy in layout_copies:
        copy.wait()
    rank_at = rank_table(layout.at[0], layout.at[1])
    k_rank[...] = rank_at(keys * side + lax.broadcasted_iota(jnp.int32, k_rank.shape, 1))

    def fill_rank(device, carry):
        q_rank[row_slab(device, tok_dev), :] = rank_at(
            device * tok_dev + lax.broadcasted_iota(jnp.int32, (tok_dev, HEAD_DIM), 0)
        )
        return carry

    lax.fori_loop(0, devices, fill_rank, 0)

    def whole_wait(view, sem):
        pltpu.make_async_copy(view, view, sem).wait()

    def slabs_of(head, count):
        return q_buf.at[head, 0 : count * tok_dev, :]

    def all_of(kind, head, which):
        return (k_buf if kind == "K" else v_buf).at[head, which, 0 : (half - 1) * tok_dev, :]

    def arrived(kind, head):
        for which in range(len(sources[kind])):
            if kind == "Q":
                arriving = devices - 1

                @pl.when(inner)
                def _():
                    whole_wait(slabs_of(head, arriving - LAYER), q_recv.at[head, 0])

                @pl.when(outer)
                def _():
                    whole_wait(slabs_of(head, arriving), q_recv.at[head, 0])

            else:
                whole_wait(all_of(kind, head, which), near_sems[kind][1].at[head, which])
            own[kind, head, which].wait()

    score_scale = 1.0 / math.sqrt(HEAD_DIM)
    block = min(tokens, 512)
    blocks = tokens // block
    per_block = block // tok_dev
    dims = (((1,), (1,)), ((), ()))
    owner_tile = 128 // tok_dev
    edge_tiles = outer_rows // 128

    def hand_out(head, target):
        send(
            o_buf.at[head, row_slab(target, tok_dev), :],
            parts_ref.at[side, :, columns(my_group * held + head)],
            o_send.at[head],
            o_recv.at[head],
            target,
        )

    def join(head):
        @pl.when(inner)
        def _():
            whole_wait(twin_lse.at[head], l_recv.at[head])
            whole_wait(twin_part.at[head], t_recv.at[head])
            for tile in range(edge_tiles):
                mine, theirs = lse[head, near_outer // owner_tile + tile], twin_lse[head, tile]
                w_mine = jnp.broadcast_to(1.0 / (1.0 + jnp.exp(theirs - mine)), (128, 128))
                w_theirs = jnp.broadcast_to(1.0 / (1.0 + jnp.exp(mine - theirs)), (128, 128))
                spot = slice(tile * 128, (tile + 1) * 128)
                full = edge_part[head, spot, :] * jnp.transpose(w_mine)
                full = full + twin_part[head, spot, :].astype(jnp.float32) * jnp.transpose(w_theirs)
                at = pl.ds(pl.multiple_of(near_outer * tok_dev + tile * 128, 128), 128)
                o_buf[head, at, :] = full.astype(jnp.bfloat16)

            def one(j, carry):
                hand_out(head, near_outer + j)
                return carry

            lax.fori_loop(0, LAYER, one, 0)


    for head in range(held):
        arrived("K", head)
        arrived("Q", head)
        start_all(ISSUE[1 + 3 * head])

        def probs_block(i, carry, head=head):
            at = row_slab(i, block)
            q = q_buf[head, at, :]
            fresh = lax.dot_general(q, k_buf[head, 0], dims, preferred_element_type=jnp.float32)
            stale = lax.dot_general(q, k_buf[head, 1], dims, preferred_element_type=jnp.float32)
            fresh_ok = k_rank[0:1, :] <= q_rank[at, 0:1]
            scores = jnp.where(fresh_ok, fresh, stale) * score_scale
            top = jnp.max(scores, axis=1, keepdims=True)
            weights = jnp.exp(scores - top)
            total = jnp.sum(weights, axis=1, keepdims=True)
            probs = weights * (1.0 / total)
            p_fresh[head, at, :] = jnp.where(fresh_ok, probs, 0.0).astype(jnp.bfloat16)
            p_stale[head, at, :] = jnp.where(fresh_ok, 0.0, probs).astype(jnp.bfloat16)
            level = jnp.broadcast_to(top + jnp.log(total), (block, 128))
            for tile in range(block // 128):
                turned = jnp.transpose(level[tile * 128 : (tile + 1) * 128, :])
                s_buf[i * (block // 128) + tile, head : head + 1, :] = turned[0:1, :]
                lse[head, i * (block // 128) + tile] = turned[0:1, :]
            return carry

        lax.fori_loop(0, blocks, probs_block, 0)
        start_all(ISSUE[2 + 3 * head])

        @pl.when(inner)
        def _(head=head):
            src = lse.at[head, pl.ds(far_outer // owner_tile, edge_tiles)]
            send(src, twin_lse.at[head], l_send.at[head], l_recv.at[head], twin)

        if head > 0:
            join(head - 1)

        if head == held - 1:

            def send_stats(step, carry):
                peer = lax.rem(me + step, devices)
                send(s_buf.at[lax.div(peer, owner_tile)], stats_ref.at[me], s_send, s_recv, peer)
                return carry

            lax.fori_loop(1, devices, send_stats, 0)

        arrived("V", head)
        start_all(ISSUE[3 + 3 * head])

        def attend_block(n, carry, head=head):
            i = lax.rem(n + (1 - side) * (blocks // 2), blocks)
            at = row_slab(i, block)
            mixed = jnp.dot(p_fresh[head, at, :], v_buf[head, 0], preferred_element_type=jnp.float32)
            mixed = mixed + jnp.dot(
                p_stale[head, at, :], v_buf[head, 1], preferred_element_type=jnp.float32
            )
            o_buf[head, at, :] = mixed.astype(jnp.bfloat16)
            near = i == side

            @pl.when(jnp.logical_and(inner, near))
            def _():
                begin = jnp.where(side == 0, 0, block - outer_rows)
                for first in (0, block - outer_rows):

                    @pl.when(begin == first)
                    def _(first=first):
                        edge_part[head] = mixed[first : first + outer_rows, :]

            @pl.when(jnp.logical_and(inner, jnp.logical_not(near)))
            def _():
                src = o_buf.at[head, row_slab(far_outer, tok_dev, LAYER), :]
                send(src, twin_part.at[head], t_send.at[head], t_recv.at[head], twin)

            def give_back(j, carry):
                target = i * per_block + j
                direct = jnp.logical_or(outer, is_inner(target, half))

                @pl.when(jnp.logical_and(target != me, direct))
                def _():
                    hand_out(head, target)

                return carry

            lax.fori_loop(0, per_block, give_back, 0)
            return carry

        lax.fori_loop(0, blocks, attend_block, 0)

    join(held - 1)
    mine = [
        pltpu.make_async_copy(
            o_buf.at[head, row_slab(me, tok_dev), :],
            parts_ref.at[side, :, columns(my_group * held + head)],
            own_sem.at[1 + head],
        )
        for head in range(held)
    ]
    mine.append(
        pltpu.make_async_copy(
            s_buf.at[lax.div(me, owner_tile)], stats_ref.at[me], own_sem.at[1 + held]
        )
    )
    for copy in mine:
        copy.start()
    s_all = stats_ref.at[0 : devices - 1]
    whole_wait(s_all, s_recv)
    mine[-1].wait()

    def levels(of_side):
        return jnp.concatenate(
            [
                stats_ref[
                    of_side * half + (head // held + of_side * LAYER) % half,
                    head % held : head % held + 1,
                    :,
                ]
                for head in range(HEADS)
            ],
            axis=0,
        )

    low, high = levels(0), levels(1)
    joined = lax.broadcasted_iota(jnp.int32, low.shape, 0) >= LAYER * held
    joined = jnp.logical_and(joined, outer)
    on_low = (side == 0).astype(jnp.float32)
    share = jnp.concatenate(
        [
            jnp.where(joined, on_low, 1.0 / (1.0 + jnp.exp(high - low))),
            jnp.where(joined, 1.0 - on_low, 1.0 / (1.0 + jnp.exp(low - high))),
            jnp.zeros((128 - 2 * HEADS, 128), jnp.float32),
        ],
        axis=0,
    )
    shares[...] = jnp.transpose(share)
    put_shares = pltpu.make_async_copy(
        shares.at[row_slab(lax.rem(me, owner_tile), tok_dev), :], shares_ref, own_sem.at[0]
    )
    put_shares.start()
    for head in range(held):
        for kind in "KV":
            for which in range(2):
                whole_wait(all_of(kind, head, which), near_sems[kind][0].at[head, which])

        @pl.when(inner)
        def _(head=head):
            whole_wait(slabs_of(head, devices - 1), q_send.at[head, 0])
            whole_wait(slabs_of(head, LAYER), pass_send.at[head])
            whole_wait(twin_lse.at[head], l_send.at[head])
            whole_wait(twin_part.at[head], t_send.at[head])

        @pl.when(outer)
        def _(head=head):
            whole_wait(slabs_of(head, devices - 1 - LAYER), q_send.at[head, 0])

    for copy in mine[:-1]:
        copy.wait()
    whole_wait(s_all, s_send)
    for head in range(held):
        most = o_buf.at[head, 0 : (devices - 1) * tok_dev, :]
        less = o_buf.at[head, 0 : (devices - 1 - LAYER) * tok_dev, :]

        @pl.when(inner)
        def _(head=head, most=most, less=less):
            whole_wait(less, o_send.at[head])
            whole_wait(most, o_recv.at[head])

        @pl.when(outer)
        def _(head=head, most=most, less=less):
            whole_wait(most, o_send.at[head])
            whole_wait(less, o_recv.at[head])

    put_shares.wait()


def merge_kernel(devices, parts, shares, out_ref, merged, out_sems):
    me = lax.axis_index("tok")
    half = devices // 2
    outer = jnp.logical_not(is_inner(me, half))
    side = lax.div(me, half)
    direct = LAYER * (HEADS // half)
    chunks = out_sems.shape[0]
    wide = HEADS // chunks
    outs = []
    for chunk in range(chunks):
        for head in range(chunk * wide, (chunk + 1) * wide):
            at = slice(head * HEAD_DIM, (head + 1) * HEAD_DIM)

            def both(at=at, head=head):
                low, high = parts[0, :, at].astype(jnp.float32), parts[1, :, at].astype(jnp.float32)
                share = shares[:, head : head + 1]
                merged[:, at] = (high + (low - high) * share).astype(jnp.bfloat16)

            if head < direct:
                both()
            else:
                pl.when(jnp.logical_not(outer))(both)

                @pl.when(outer)
                def _(at=at):
                    merged[:, at] = parts[side, :, at]

        span = pl.ds(chunk * wide * HEAD_DIM, wide * HEAD_DIM)
        out = pltpu.make_async_copy(merged.at[:, span], out_ref.at[:, span], out_sems.at[chunk])
        out.start()
        outs.append(out)
    for out in outs:
        out.wait()


def halves(*arrays):
    arrays = [pltpu.with_memory_space_constraint(array, pltpu.HBM) for array in arrays]
    queries, fresh_keys, fresh_values, stale_keys, stale_values, patch_starts, order_starts = arrays
    devices = lax.axis_size("tok")
    tok_dev, width = queries.shape
    half = devices // 2
    held = HEADS // half
    tokens, keys = devices * tok_dev, half * tok_dev
    anywhere = pl.BlockSpec(memory_space=pl.ANY)
    main_memory = pl.BlockSpec(memory_space=pltpu.HBM)
    near_memory = pl.BlockSpec(memory_space=pltpu.VMEM)
    patches = patch_starts.shape[0]
    dma = pltpu.SemaphoreType.DMA
    parts, shares = pl.pallas_call(
        functools.partial(halves_kernel, devices),
        out_shape=(
            jax.ShapeDtypeStruct((2, tok_dev, width), jnp.bfloat16),
            jax.ShapeDtypeStruct((tok_dev, 128), jnp.float32),
        ),
        in_specs=[main_memory] * 7,
        out_specs=(anywhere, anywhere),
        scratch_shapes=[
            pltpu.VMEM((held, tokens, HEAD_DIM), jnp.bfloat16),
            pltpu.VMEM((held, 2, keys, HEAD_DIM), jnp.bfloat16),
            pltpu.VMEM((held, 2, keys, HEAD_DIM), jnp.bfloat16),
            pltpu.VMEM((held, tokens, keys), jnp.bfloat16),
            pltpu.VMEM((held, tokens, keys), jnp.bfloat16),
            pltpu.VMEM((held, tokens, HEAD_DIM), jnp.bfloat16),
            pltpu.VMEM((tokens // 128, held, 128), jnp.float32),
            pltpu.VMEM((devices, held, 128), jnp.float32),
            pltpu.VMEM((128, 128), jnp.float32),
            pltpu.VMEM((tokens, HEAD_DIM), jnp.int32),
            pltpu.VMEM((8, keys), jnp.int32),
            dma((held, 1)),
            dma((held, 2)),
            dma((held, 2)),
            dma((held, 2)),
            dma((held, 2)),
            dma((held, 2)),
            dma((5 * held,)),
            dma((held,)),
            dma((held,)),
            dma,
            dma,
            pltpu.SemaphoreType.REGULAR,
            pltpu.SMEM((2, patches), jnp.int32),
            dma((2,)),
            pltpu.VMEM((held, tokens // 128, 1, 128), jnp.float32),
            pltpu.VMEM((held, LAYER * tok_dev // 128, 1, 128), jnp.float32),
            pltpu.VMEM((held, LAYER * tok_dev, HEAD_DIM), jnp.bfloat16),
            pltpu.VMEM((held, LAYER * tok_dev, HEAD_DIM), jnp.float32),
            dma((held,)),
            dma((held,)),
            dma((held,)),
            dma((held,)),
            dma((held,)),
        ],
        compiler_params=pltpu.CompilerParams(
            collective_id=0, has_side_effects=True, vmem_limit_bytes=32 * 1024 * 1024
        ),
    )(patch_starts, order_starts, queries, fresh_keys, stale_keys, fresh_values, stale_values)
    return pl.pallas_call(
        functools.partial(merge_kernel, devices),
        out_shape=jax.ShapeDtypeStruct((tok_dev, width), jnp.bfloat16),
        in_specs=[near_memory, near_memory],
        out_specs=main_memory,
        scratch_shapes=[pltpu.VMEM((tok_dev, width), jnp.bfloat16), dma((2,))],
        compiler_params=pltpu.CompilerParams(vmem_limit_bytes=16 * 1024 * 1024),
    )(parts, shares)


def solution(mesh):
    placed = (P(("groups", "tok"), None),) * 5 + (P("groups"),) * 2
    devices = mesh.shape["tok"]

    def body(*arrays):
        tok_dev = arrays[0].shape[0]
        split = devices % 2 == 0 and HEADS % (devices // 2) == 0
        split = split and devices // 2 == 2 * LAYER and LAYER * tok_dev % 128 == 0
        split = split and 2 * LAYER * tok_dev == 512
        split = split and 128 % tok_dev == 0 and devices * tok_dev % 512 == 0
        return (halves if split else shards)(*arrays)

    return jax.shard_map(
        body, mesh=mesh, in_specs=placed, out_specs=P(("groups", "tok"), None), check_vma=False
    )
```

```python
import functools
import math

import jax
import jax.numpy as jnp
from jax import lax
from jax.experimental import pallas as pl
from jax.experimental.pallas import tpu as pltpu
from jax.sharding import PartitionSpec as P

HEADS = 16
HEAD_DIM = 128
LAYER = 4
ISSUE = ((('Q', 0, ('cross', 'beside'), None), ('K', 0, ('cross', 'beside'), None), ('ready', 0, (), None), ('Q', 0, ('far',), None), ('V', 0, ('cross', 'beside'), None), ('Q', 1, ('cross',), 'outer'), ('Q', 1, ('beside',), None), ('pass', 0, (), None), ('Q', 1, ('far',), None), ('K', 1, ('cross', 'beside'), None), ('V', 1, ('cross', 'beside'), None)), (('Q', 1, ('cross',), 'inner'),), (('pass', 1, (), None),), (), (), (), ())
HELD_BACK = (0, 1)
MESH = pl.DeviceIdType.MESH


def attention_kernel(
    devices,
    patch_starts,
    order_starts,
    queries,
    fresh_keys,
    stale_keys,
    fresh_values,
    stale_values,
    out_ref,
    q_buf,
    kv_buf,
    p_fresh,
    p_stale,
    o_buf,
    q_rank,
    k_rank,
    send_sems,
    recv_sems,
    own_sem,
    out_send,
    out_recv,
):
    me = lax.axis_index("tok")
    tok_dev = queries.shape[0]
    group_size = devices // HEADS
    slab = tok_dev // group_size
    tokens = devices * tok_dev
    rows = devices * slab
    my_head = me // group_size
    my_member = me % group_size
    barrier = pltpu.get_barrier_semaphore()

    def peer_of(step):
        return lax.rem(me + step, devices)

    def columns(head):
        return pl.ds(pl.multiple_of(head * HEAD_DIM, HEAD_DIM), HEAD_DIM)

    def row_slab(index, size):
        return pl.ds(pl.multiple_of(index * size, size), size)

    def greet(step, carry):
        pl.semaphore_signal(barrier, inc=1, device_id={"tok": peer_of(step)}, device_id_type=MESH)
        return carry

    lax.fori_loop(1, devices, greet, 0)

    sources = (queries, fresh_keys, stale_keys, fresh_values, stale_values)

    def source_view(which, device):
        head, member = device // group_size, device % group_size
        if which == 0:
            return queries.at[row_slab(member, slab), columns(head)]
        return sources[which].at[:, columns(head)]

    def landing(which, device):
        if which == 0:
            return q_buf.at[row_slab(device, slab), :]
        return kv_buf.at[which - 1, row_slab(device, tok_dev), :]

    own = [
        pltpu.make_async_copy(source_view(which, me), landing(which, me), own_sem.at[which])
        for which in range(5)
    ]
    for copy in own:
        copy.start()
    pl.semaphore_wait(barrier, devices - 1)

    for which in range(5):

        def send(step, carry, which=which):
            peer = peer_of(step)
            pltpu.make_async_remote_copy(
                src_ref=source_view(which, peer),
                dst_ref=landing(which, me),
                send_sem=send_sems.at[which],
                recv_sem=recv_sems.at[which],
                device_id={"tok": peer},
                device_id_type=MESH,
            ).start()
            return carry

        lax.fori_loop(1, devices, send, 0)

    patches = patch_starts.shape[0]
    starts = [patch_starts[p] for p in range(patches)]
    orders = [order_starts[p] for p in range(patches)]
    ranks = []
    for p in range(patches):
        rank = jnp.int32(0)
        for i in range(patches):
            rank = rank + jnp.where(orders[i] == starts[p], jnp.int32(i), jnp.int32(0))
        ranks.append(rank)
    jumps = [ranks[0]] + [ranks[p] - ranks[p - 1] for p in range(1, patches)]

    def rank_at(positions):
        total = jnp.zeros(positions.shape, jnp.int32)
        for p in range(patches):
            total = total + jnp.where(positions >= starts[p], jumps[p], 0)
        return total

    k_rank[...] = rank_at(lax.broadcasted_iota(jnp.int32, k_rank.shape, 1))

    def fill_rank(device, carry):
        base = device * tok_dev + my_member * slab
        q_rank[row_slab(device, slab), :] = rank_at(
            base + lax.broadcasted_iota(jnp.int32, (slab, HEAD_DIM), 0)
        )
        return carry

    lax.fori_loop(0, devices, fill_rank, 0)

    def all_of(which):
        size = (devices - 1) * (slab if which == 0 else tok_dev)
        return q_buf.at[0:size, :] if which == 0 else kv_buf.at[which - 1, 0:size, :]

    def arrived(which):
        view = all_of(which)
        pltpu.make_async_copy(view, view, recv_sems.at[which]).wait()
        own[which].wait()

    for which in range(3):
        arrived(which)

    score_scale = 1.0 / math.sqrt(HEAD_DIM)
    block = max(slab, min(rows, (1 << 18) // tokens))
    blocks = rows // block
    dims = (((1,), (1,)), ((), ()))

    def probs_block(i, carry):
        at = row_slab(i, block)
        q = q_buf[at, :]
        fresh = lax.dot_general(q, kv_buf[0], dims, preferred_element_type=jnp.float32)
        stale = lax.dot_general(q, kv_buf[1], dims, preferred_element_type=jnp.float32)
        fresh_ok = k_rank[0:1, :] <= q_rank[at, 0:1]
        scores = jnp.where(fresh_ok, fresh, stale) * score_scale
        top = jnp.max(scores, axis=1, keepdims=True)
        weights = jnp.exp(scores - top)
        total = jnp.sum(weights, axis=1, keepdims=True)
        probs = weights * (1.0 / total)
        p_fresh[at, :] = jnp.where(fresh_ok, probs, 0.0).astype(jnp.bfloat16)
        p_stale[at, :] = jnp.where(fresh_ok, 0.0, probs).astype(jnp.bfloat16)
        return carry

    lax.fori_loop(0, blocks, probs_block, 0)

    for which in range(3, 5):
        arrived(which)

    per_block = block // slab

    def give_back(i):
        def one(j, carry):
            target = i * per_block + j

            @pl.when(target != me)
            def _():
                pltpu.make_async_remote_copy(
                    src_ref=o_buf.at[row_slab(target, slab), :],
                    dst_ref=out_ref.at[row_slab(my_member, slab), columns(my_head)],
                    send_sem=out_send,
                    recv_sem=out_recv,
                    device_id={"tok": target},
                    device_id_type=MESH,
                ).start()

            return carry

        lax.fori_loop(0, per_block, one, 0)

    def attend_block(i, carry):
        at = row_slab(i, block)
        mixed = jnp.dot(p_fresh[at, :], kv_buf[2], preferred_element_type=jnp.float32)
        mixed = mixed + jnp.dot(p_stale[at, :], kv_buf[3], preferred_element_type=jnp.float32)
        o_buf[at, :] = mixed.astype(jnp.bfloat16)
        give_back(i)
        return carry

    lax.fori_loop(0, blocks, attend_block, 0)
    mine = pltpu.make_async_copy(
        o_buf.at[row_slab(me, slab), :],
        out_ref.at[row_slab(my_member, slab), columns(my_head)],
        own_sem.at[0],
    )
    mine.start()
    for which in range(5):
        view = all_of(which)
        pltpu.make_async_copy(view, view, send_sems.at[which]).wait()
    view = o_buf.at[0 : (devices - 1) * slab, :]
    mine.wait()
    pltpu.make_async_copy(view, view, out_send).wait()
    pltpu.make_async_copy(view, view, out_recv).wait()


def shards(queries, fresh_keys, fresh_values, stale_keys, stale_values, patch_starts, order_starts):
    devices = lax.axis_size("tok")
    tok_dev, width = queries.shape
    slab = tok_dev // (devices // HEADS)
    tokens, rows = devices * tok_dev, devices * slab
    anywhere = pl.BlockSpec(memory_space=pl.ANY)
    scalars = pl.BlockSpec(memory_space=pltpu.SMEM)
    return pl.pallas_call(
        functools.partial(attention_kernel, devices),
        out_shape=jax.ShapeDtypeStruct((tok_dev, width), jnp.bfloat16),
        in_specs=[scalars] * 2 + [anywhere] * 5,
        out_specs=anywhere,
        scratch_shapes=[
            pltpu.VMEM((rows, HEAD_DIM), jnp.bfloat16),
            pltpu.VMEM((4, tokens, HEAD_DIM), jnp.bfloat16),
            pltpu.VMEM((rows, tokens), jnp.bfloat16),
            pltpu.VMEM((rows, tokens), jnp.bfloat16),
            pltpu.VMEM((rows, HEAD_DIM), jnp.bfloat16),
            pltpu.VMEM((rows, HEAD_DIM), jnp.int32),
            pltpu.VMEM((8, tokens), jnp.int32),
            pltpu.SemaphoreType.DMA((5,)),
            pltpu.SemaphoreType.DMA((5,)),
            pltpu.SemaphoreType.DMA((5,)),
            pltpu.SemaphoreType.DMA,
            pltpu.SemaphoreType.DMA,
        ],
        compiler_params=pltpu.CompilerParams(
            collective_id=0, has_side_effects=True, vmem_limit_bytes=60 * 1024 * 1024
        ),
    )(
        patch_starts,
        order_starts,
        queries,
        fresh_keys,
        stale_keys,
        fresh_values,
        stale_values,
    )


def rank_table(patch_starts, order_starts):
    patches = patch_starts.shape[0]
    starts = [patch_starts[p] for p in range(patches)]
    orders = [order_starts[p] for p in range(patches)]
    ranks = []
    for p in range(patches):
        rank = jnp.int32(0)
        for i in range(patches):
            rank = rank + jnp.where(orders[i] == starts[p], jnp.int32(i), jnp.int32(0))
        ranks.append(rank)
    jumps = [ranks[0]] + [ranks[p] - ranks[p - 1] for p in range(1, patches)]

    def rank_at(positions):
        total = jnp.zeros(positions.shape, jnp.int32)
        for p in range(patches):
            total = total + jnp.where(positions >= starts[p], jumps[p], 0)
        return total

    return rank_at


def seat(device, half):
    shift = jnp.where(device >= half, LAYER, 0)
    return lax.rem(lax.rem(device, half) + shift, half)


def is_inner(device, half):
    return seat(device, half) >= LAYER


def halves_kernel(
    devices,
    starts_in,
    orders_in,
    queries,
    fresh_keys,
    stale_keys,
    fresh_values,
    stale_values,
    parts_ref,
    shares_ref,
    q_buf,
    k_buf,
    v_buf,
    p_fresh,
    p_stale,
    o_buf,
    stats,
    shares,
    q_rank,
    k_rank,
    sent,
    q_recv,
    k_recv,
    v_recv,
    o_recv,
    s_send,
    s_recv,
    ready,
    layout,
    layout_sem,
    lse,
    twin_lse,
    twin_part,
    edge_part,
    l_send,
    l_recv,
    t_recv,
):
    me = lax.axis_index("tok")
    tok_dev = queries.shape[0]
    half = devices // 2
    held = HEADS // half
    tokens = devices * tok_dev
    keys = half * tok_dev
    side, place = lax.div(me, half), lax.rem(me, half)
    outer_rows = LAYER * tok_dev
    my_group = seat(me, half)
    inner = my_group >= LAYER
    outer = jnp.logical_not(inner)
    plane = lax.div(me, LAYER)
    other_plane = plane + 1 - 2 * lax.rem(plane, 2)
    outward = jnp.where(side == 0, -LAYER, LAYER)
    twin = me - outward
    near_outer = jnp.where(side == 0, 0, devices - LAYER)
    far_outer = devices - LAYER - near_outer
    barrier = pltpu.get_barrier_semaphore()

    def near_peer(step):
        return side * half + lax.rem(place + step, half)

    def far_peer(step):
        return (1 - side) * half + lax.rem(place + step, half)

    def columns(head):
        return pl.ds(pl.multiple_of(head * HEAD_DIM, HEAD_DIM), HEAD_DIM)

    def row_slab(index, size, count=1):
        return pl.ds(pl.multiple_of(index * size, size), size * count)

    def signal(sem, device):
        pl.semaphore_signal(sem, inc=1, device_id={"tok": device}, device_id_type=MESH)

    def greet(step, carry):
        signal(barrier, near_peer(step))
        return carry

    @pl.when(inner)
    def _():
        signal(barrier, twin)

    lax.fori_loop(1, half, greet, 0)
    layout_copies = [
        pltpu.make_async_copy(whole, layout.at[n], layout_sem.at[n])
        for n, whole in enumerate((starts_in, orders_in))
    ]
    for copy in layout_copies:
        copy.start()

    def send(src, dst, send_sem, recv_sem, device):
        pltpu.make_async_remote_copy(
            src_ref=src,
            dst_ref=dst,
            send_sem=send_sem,
            recv_sem=recv_sem,
            device_id={"tok": device},
            device_id_type=MESH,
        ).start()

    sources = {"Q": (queries,), "K": (fresh_keys, stale_keys), "V": (fresh_values, stale_values)}
    def landed(kind, head):
        if kind == "Q":
            return q_recv.at[head, plane]
        return (k_recv if kind == "K" else v_recv).at[head]


    def landing(kind, head, which):
        if kind == "Q":
            return q_buf.at[head, row_slab(me, tok_dev), :]
        return (k_buf if kind == "K" else v_buf).at[head, which, row_slab(place, tok_dev), :]

    def source(kind, head, which, device):
        return sources[kind][which].at[:, columns(head * half + seat(device, half))]

    def share_out(kind, head, spread):
        def go(step, peer):
            for which in range(len(sources[kind])):
                send(
                    source(kind, head, which, peer),
                    landing(kind, head, which),
                    sent,
                    landed(kind, head),
                    peer,
                )

        def cross(step, carry):
            go(step, other_plane * LAYER + lax.rem(me + step, LAYER))
            return carry

        def beside(step, carry):
            go(step, plane * LAYER + lax.rem(me + step, LAYER))
            return carry

        def far(step, carry):
            peer = far_peer(step)
            pl.when(jnp.logical_or(inner, jnp.logical_not(is_inner(peer, half))))(
                lambda: go(step, peer)
            )
            return carry

        if "cross" in spread:
            lax.fori_loop(0, LAYER, cross, 0)
        if "beside" in spread:
            lax.fori_loop(1, LAYER, beside, 0)
        if "far" in spread:
            lax.fori_loop(0, half, far, 0)

    def pass_on(head):
        @pl.when(inner)
        def _():
            view = q_buf.at[head, row_slab(near_outer, tok_dev, LAYER), :]
            pltpu.make_async_copy(view, view, q_recv.at[head, other_plane]).wait()
            send(view, view, sent, q_recv.at[head, other_plane], twin)

    def start_all(steps):
        for kind, head, spread, who in steps:
            if kind == "pass":
                pass_on(head)
            elif kind == "ready":
                pl.semaphore_wait(ready, 1)

                @pl.when(inner)
                def _():
                    signal(ready, me + outward)

            elif who is not None:
                pl.when(inner if who == "inner" else outer)(
                    lambda kind=kind, head=head, spread=spread: share_out(kind, head, spread)
                )
            else:
                share_out(kind, head, spread)

    pl.semaphore_wait(barrier, half - 1 + inner.astype(jnp.int32))

    @pl.when(inner)
    def _():
        signal(ready, twin)

    start_all(ISSUE[0])

    for head in range(held):
        for kind in "QKV":
            for which in range(len(sources[kind])):
                pltpu.make_async_copy(
                    source(kind, head, which, me), landing(kind, head, which), landed(kind, head)
                ).start()

    for copy in layout_copies:
        copy.wait()
    rank_at = rank_table(layout.at[0], layout.at[1])
    k_rank[...] = rank_at(keys * side + lax.broadcasted_iota(jnp.int32, k_rank.shape, 1))

    def fill_rank(device, carry):
        q_rank[row_slab(device, tok_dev), :] = rank_at(
            device * tok_dev + lax.broadcasted_iota(jnp.int32, (tok_dev, HEAD_DIM), 0)
        )
        return carry

    lax.fori_loop(0, devices, fill_rank, 0)

    def whole_wait(view, sem):
        pltpu.make_async_copy(view, view, sem).wait()

    def arrived(kind, head):
        whole_wait((k_buf if kind == "K" else v_buf).at[head], landed(kind, head))

    def asked(head, i):
        @pl.when(jnp.logical_not(jnp.logical_and(inner, i == other_plane)))
        def _():
            whole_wait(q_buf.at[head, row_slab(i, outer_rows), :], q_recv.at[head, i])

    score_scale = 1.0 / math.sqrt(HEAD_DIM)
    block = outer_rows
    dims = (((1,), (1,)), ((), ()))
    owner_tile = 128 // tok_dev
    edge_tiles = outer_rows // 128

    def plane_order(n):
        last = devices // LAYER - 1
        swapped = jnp.where(n >= 2, 5 - n, n)
        return jnp.where(side == 0, last - swapped, swapped)

    def send_levels(head, i):
        def one(j, carry):
            target = i * LAYER + j

            @pl.when(target != me)
            def _():
                src = lse.at[head, lax.div(target, owner_tile)]
                send(src, stats.at[head, me], s_send, s_recv.at[head], target)

            return carry

        lax.fori_loop(0, LAYER, one, 0)

        @pl.when(jnp.logical_and(inner, i * LAYER == far_outer))
        def _():
            src = lse.at[head, pl.ds(far_outer // owner_tile, edge_tiles)]
            send(src, twin_lse.at[head], l_send, l_recv.at[head], twin)

    def hand_out(head, target):
        send(
            o_buf.at[head, row_slab(target, tok_dev), :],
            parts_ref.at[side, :, columns(head * half + my_group)],
            sent,
            o_recv.at[head],
            target,
        )

    def join(head):
        @pl.when(inner)
        def _():
            whole_wait(twin_lse.at[head], l_recv.at[head])
            whole_wait(twin_part.at[head], t_recv.at[head])
            for tile in range(edge_tiles):
                mine, theirs = lse[head, near_outer // owner_tile + tile], twin_lse[head, tile]
                w_mine = jnp.broadcast_to(1.0 / (1.0 + jnp.exp(theirs - mine)), (128, 128))
                w_theirs = jnp.broadcast_to(1.0 / (1.0 + jnp.exp(mine - theirs)), (128, 128))
                spot = slice(tile * 128, (tile + 1) * 128)
                full = edge_part[head, spot, :] * jnp.transpose(w_mine)
                full = full + twin_part[head, spot, :].astype(jnp.float32) * jnp.transpose(w_theirs)
                at = pl.ds(pl.multiple_of(near_outer * tok_dev + tile * 128, 128), 128)
                o_buf[head, at, :] = full.astype(jnp.bfloat16)

            def one(j, carry):
                hand_out(head, near_outer + j)
                return carry

            lax.fori_loop(0, LAYER, one, 0)


    for head in range(held):
        arrived("K", head)
        start_all(ISSUE[1 + 3 * head])

        def probs_block(n, carry, head=head):
            i = plane_order(n)
            asked(head, i)
            at = row_slab(i, block)
            q = q_buf[head, at, :]
            fresh = lax.dot_general(q, k_buf[head, 0], dims, preferred_element_type=jnp.float32)
            stale = lax.dot_general(q, k_buf[head, 1], dims, preferred_element_type=jnp.float32)
            fresh_ok = k_rank[0:1, :] <= q_rank[at, 0:1]
            scores = jnp.where(fresh_ok, fresh, stale) * score_scale
            top = jnp.max(scores, axis=1, keepdims=True)
            weights = jnp.exp(scores - top)
            total = jnp.sum(weights, axis=1, keepdims=True)
            probs = weights * (1.0 / total)
            p_fresh[head, at, :] = jnp.where(fresh_ok, probs, 0.0).astype(jnp.bfloat16)
            p_stale[head, at, :] = jnp.where(fresh_ok, 0.0, probs).astype(jnp.bfloat16)
            level = jnp.broadcast_to(top + jnp.log(total), (block, 128))
            for tile in range(block // 128):
                turned = jnp.transpose(level[tile * 128 : (tile + 1) * 128, :])
                lse[head, i * (block // 128) + tile] = turned[0:1, :]
            send_levels(head, i)
            return carry

        def attend_block(n, carry, head=head):
            i = plane_order(n)
            at = row_slab(i, outer_rows)
            mixed = jnp.dot(p_fresh[head, at, :], v_buf[head, 0], preferred_element_type=jnp.float32)
            mixed = mixed + jnp.dot(
                p_stale[head, at, :], v_buf[head, 1], preferred_element_type=jnp.float32
            )
            o_buf[head, at, :] = mixed.astype(jnp.bfloat16)

            @pl.when(jnp.logical_and(inner, i * LAYER == near_outer))
            def _():
                edge_part[head] = mixed

            @pl.when(jnp.logical_and(inner, i * LAYER == far_outer))
            def _():
                src = o_buf.at[head, row_slab(far_outer, tok_dev, LAYER), :]
                send(src, twin_part.at[head], sent, t_recv.at[head], twin)

            def give_back(j, carry):
                target = i * LAYER + j
                direct = jnp.logical_or(outer, is_inner(target, half))

                @pl.when(jnp.logical_and(target != me, direct))
                def _():
                    hand_out(head, target)

                return carry

            lax.fori_loop(0, LAYER, give_back, 0)
            return carry

        if head > 0:
            join(head - 1)
        planes = devices // LAYER
        early = planes - HELD_BACK[head]
        lax.fori_loop(0, early, probs_block, 0)
        start_all(ISSUE[2 + 3 * head])
        arrived("V", head)
        start_all(ISSUE[3 + 3 * head])
        lax.fori_loop(0, early, attend_block, 0)
        if early < planes:
            lax.fori_loop(early, planes, probs_block, 0)
            lax.fori_loop(early, planes, attend_block, 0)

    join(held - 1)
    for head in range(held):
        pltpu.make_async_copy(
            o_buf.at[head, row_slab(me, tok_dev), :],
            parts_ref.at[side, :, columns(head * half + my_group)],
            o_recv.at[head],
        ).start()
        pltpu.make_async_copy(
            lse.at[head, lax.div(me, owner_tile)], stats.at[head, me], s_recv.at[head]
        ).start()

    def outputs_in(head):
        @pl.when(inner)
        def _():
            whole_wait(o_buf.at[head], o_recv.at[head])

        @pl.when(outer)
        def _():
            whole_wait(o_buf.at[head, 0 : (devices - LAYER) * tok_dev, :], o_recv.at[head])

    for head in range(held):
        whole_wait(stats.at[head], s_recv.at[head])

        def levels(of_side, head=head):
            return jnp.concatenate(
                [
                    stats[head, of_side * half + (group + of_side * LAYER) % half]
                    for group in range(half)
                ],
                axis=0,
            )

        share = 1.0 / (1.0 + jnp.exp(levels(1) - levels(0)))
        share = jnp.concatenate([share, jnp.zeros((128 - half, 128), jnp.float32)], axis=0)
        shares[...] = jnp.transpose(share)
        rows = row_slab(lax.rem(me, owner_tile), tok_dev)
        if head < held - 1:
            outputs_in(head)
            merge_slot(head, half, parts_ref, shares.at[rows, :], outer, side, parts_ref.at[0])
        else:
            shares_ref[...] = shares[rows, :]

    outputs_in(held - 1)
    whole_wait(stats.at[:, 0 : devices - 1], s_send)
    slab = tok_dev * HEAD_DIM

    def all_sent(slabs):
        whole_wait(p_fresh.at[:, 0 : slabs * slab // keys, :], sent)

    kv, out = 4 * (half - 1), devices - 1

    @pl.when(inner)
    def _():
        whole_wait(twin_lse, l_send)
        all_sent(kv + devices - 1 + LAYER + out)

    @pl.when(outer)
    def _():
        all_sent(kv + devices - 1 - LAYER + out)


def merge_slot(slot, half, parts, shares, outer, side, out):
    for head in range(slot * half, (slot + 1) * half):
        at = slice(head * HEAD_DIM, (head + 1) * HEAD_DIM)

        def both(at=at, head=head):
            low, high = parts[0, :, at].astype(jnp.float32), parts[1, :, at].astype(jnp.float32)
            share = shares[:, head % half : head % half + 1]
            out[:, at] = (high + (low - high) * share).astype(jnp.bfloat16)

        if head % half < LAYER:
            both()
        else:
            pl.when(jnp.logical_not(outer))(both)

            @pl.when(outer)
            def _(at=at):
                out[:, at] = parts[side, :, at]


def merge_kernel(devices, parts, shares, out_ref, merged, out_sems):
    half = devices // 2
    me = lax.axis_index("tok")
    last = HEADS // half - 1
    done = last * half * HEAD_DIM
    early = pltpu.make_async_copy(
        parts.at[0, :, 0:done], out_ref.at[:, 0:done], out_sems.at[0]
    )
    early.start()
    outer = jnp.logical_not(is_inner(me, half))
    merge_slot(last, half, parts, shares, outer, lax.div(me, half), merged)
    late = pltpu.make_async_copy(merged.at[:, done:], out_ref.at[:, done:], out_sems.at[1])
    late.start()
    early.wait()
    late.wait()


def halves(*arrays):
    arrays = [pltpu.with_memory_space_constraint(array, pltpu.HBM) for array in arrays]
    queries, fresh_keys, fresh_values, stale_keys, stale_values, patch_starts, order_starts = arrays
    devices = lax.axis_size("tok")
    tok_dev, width = queries.shape
    half = devices // 2
    held = HEADS // half
    tokens, keys = devices * tok_dev, half * tok_dev
    anywhere = pl.BlockSpec(memory_space=pl.ANY)
    main_memory = pl.BlockSpec(memory_space=pltpu.HBM)
    near_memory = pl.BlockSpec(memory_space=pltpu.VMEM)
    patches = patch_starts.shape[0]
    dma = pltpu.SemaphoreType.DMA
    parts, shares = pl.pallas_call(
        functools.partial(halves_kernel, devices),
        out_shape=(
            jax.ShapeDtypeStruct((2, tok_dev, width), jnp.bfloat16),
            jax.ShapeDtypeStruct((tok_dev, 128), jnp.float32),
        ),
        in_specs=[main_memory] * 7,
        out_specs=(near_memory, near_memory),
        scratch_shapes=[
            pltpu.VMEM((held, tokens, HEAD_DIM), jnp.bfloat16),
            pltpu.VMEM((held, 2, keys, HEAD_DIM), jnp.bfloat16),
            pltpu.VMEM((held, 2, keys, HEAD_DIM), jnp.bfloat16),
            pltpu.VMEM((held, tokens, keys), jnp.bfloat16),
            pltpu.VMEM((held, tokens, keys), jnp.bfloat16),
            pltpu.VMEM((held, tokens, HEAD_DIM), jnp.bfloat16),
            pltpu.VMEM((held, devices, 1, 128), jnp.float32),
            pltpu.VMEM((128, 128), jnp.float32),
            pltpu.VMEM((tokens, HEAD_DIM), jnp.int32),
            pltpu.VMEM((8, keys), jnp.int32),
            dma,
            dma((held, devices // LAYER)),
            dma((held,)),
            dma((held,)),
            dma((held,)),
            dma,
            dma((held,)),
            pltpu.SemaphoreType.REGULAR,
            pltpu.SMEM((2, patches), jnp.int32),
            dma((2,)),
            pltpu.VMEM((held, tokens // 128, 1, 128), jnp.float32),
            pltpu.VMEM((held, LAYER * tok_dev // 128, 1, 128), jnp.float32),
            pltpu.VMEM((held, LAYER * tok_dev, HEAD_DIM), jnp.bfloat16),
            pltpu.VMEM((held, LAYER * tok_dev, HEAD_DIM), jnp.float32),
            dma,
            dma((held,)),
            dma((held,)),
        ],
        compiler_params=pltpu.CompilerParams(
            collective_id=0, has_side_effects=True, vmem_limit_bytes=32 * 1024 * 1024
        ),
    )(patch_starts, order_starts, queries, fresh_keys, stale_keys, fresh_values, stale_values)
    return pl.pallas_call(
        functools.partial(merge_kernel, devices),
        out_shape=jax.ShapeDtypeStruct((tok_dev, width), jnp.bfloat16),
        in_specs=[near_memory, near_memory],
        out_specs=main_memory,
        scratch_shapes=[pltpu.VMEM((tok_dev, width), jnp.bfloat16), dma((2,))],
        compiler_params=pltpu.CompilerParams(vmem_limit_bytes=16 * 1024 * 1024),
    )(parts, shares)


def solution(mesh):
    placed = (P(("groups", "tok"), None),) * 5 + (P("groups"),) * 2
    devices = mesh.shape["tok"]

    def body(*arrays):
        tok_dev = arrays[0].shape[0]
        split = devices % 2 == 0 and HEADS % (devices // 2) == 0
        split = split and devices // 2 == 2 * LAYER and LAYER * tok_dev % 128 == 0
        split = split and 2 * LAYER * tok_dev == 512
        split = split and 128 % tok_dev == 0 and devices * tok_dev % 512 == 0
        return (halves if split else shards)(*arrays)

    return jax.shard_map(
        body, mesh=mesh, in_specs=placed, out_specs=P(("groups", "tok"), None), check_vma=False
    )
```

```python
import functools
import math

import jax
import jax.numpy as jnp
from jax import lax
from jax.experimental import pallas as pl
from jax.experimental.pallas import tpu as pltpu
from jax.sharding import PartitionSpec as P

HEADS = 16
HEAD_DIM = 128
LAYER = 4
ISSUE = ((('Q', 0, ('cross', 'beside'), None), ('K', 0, ('cross', 'beside'), None), ('ready', 0, (), None), ('Q', 0, ('far',), None), ('V', 0, ('cross', 'beside'), None), ('Q', 1, ('cross',), 'outer'), ('Q', 1, ('beside',), None), ('pass', 0, (), None), ('Q', 1, ('far',), None), ('K', 1, ('cross', 'beside'), None), ('V', 1, ('cross', 'beside'), None)), (('Q', 1, ('cross',), 'inner'),), (('pass', 1, (), None),), (), (), (), ())
HELD_BACK = (0, 1)
MESH = pl.DeviceIdType.MESH


def attention_kernel(
    devices,
    patch_starts,
    order_starts,
    queries,
    fresh_keys,
    stale_keys,
    fresh_values,
    stale_values,
    out_ref,
    q_buf,
    kv_buf,
    p_fresh,
    p_stale,
    o_buf,
    q_rank,
    k_rank,
    send_sems,
    recv_sems,
    own_sem,
    out_send,
    out_recv,
):
    me = lax.axis_index("tok")
    tok_dev = queries.shape[0]
    group_size = devices // HEADS
    slab = tok_dev // group_size
    tokens = devices * tok_dev
    rows = devices * slab
    my_head = me // group_size
    my_member = me % group_size
    barrier = pltpu.get_barrier_semaphore()

    def peer_of(step):
        return lax.rem(me + step, devices)

    def columns(head):
        return pl.ds(pl.multiple_of(head * HEAD_DIM, HEAD_DIM), HEAD_DIM)

    def row_slab(index, size):
        return pl.ds(pl.multiple_of(index * size, size), size)

    def greet(step, carry):
        pl.semaphore_signal(barrier, inc=1, device_id={"tok": peer_of(step)}, device_id_type=MESH)
        return carry

    lax.fori_loop(1, devices, greet, 0)

    sources = (queries, fresh_keys, stale_keys, fresh_values, stale_values)

    def source_view(which, device):
        head, member = device // group_size, device % group_size
        if which == 0:
            return queries.at[row_slab(member, slab), columns(head)]
        return sources[which].at[:, columns(head)]

    def landing(which, device):
        if which == 0:
            return q_buf.at[row_slab(device, slab), :]
        return kv_buf.at[which - 1, row_slab(device, tok_dev), :]

    own = [
        pltpu.make_async_copy(source_view(which, me), landing(which, me), own_sem.at[which])
        for which in range(5)
    ]
    for copy in own:
        copy.start()
    pl.semaphore_wait(barrier, devices - 1)

    for which in range(5):

        def send(step, carry, which=which):
            peer = peer_of(step)
            pltpu.make_async_remote_copy(
                src_ref=source_view(which, peer),
                dst_ref=landing(which, me),
                send_sem=send_sems.at[which],
                recv_sem=recv_sems.at[which],
                device_id={"tok": peer},
                device_id_type=MESH,
            ).start()
            return carry

        lax.fori_loop(1, devices, send, 0)

    patches = patch_starts.shape[0]
    starts = [patch_starts[p] for p in range(patches)]
    orders = [order_starts[p] for p in range(patches)]
    ranks = []
    for p in range(patches):
        rank = jnp.int32(0)
        for i in range(patches):
            rank = rank + jnp.where(orders[i] == starts[p], jnp.int32(i), jnp.int32(0))
        ranks.append(rank)
    jumps = [ranks[0]] + [ranks[p] - ranks[p - 1] for p in range(1, patches)]

    def rank_at(positions):
        total = jnp.zeros(positions.shape, jnp.int32)
        for p in range(patches):
            total = total + jnp.where(positions >= starts[p], jumps[p], 0)
        return total

    k_rank[...] = rank_at(lax.broadcasted_iota(jnp.int32, k_rank.shape, 1))

    def fill_rank(device, carry):
        base = device * tok_dev + my_member * slab
        q_rank[row_slab(device, slab), :] = rank_at(
            base + lax.broadcasted_iota(jnp.int32, (slab, HEAD_DIM), 0)
        )
        return carry

    lax.fori_loop(0, devices, fill_rank, 0)

    def all_of(which):
        size = (devices - 1) * (slab if which == 0 else tok_dev)
        return q_buf.at[0:size, :] if which == 0 else kv_buf.at[which - 1, 0:size, :]

    def arrived(which):
        view = all_of(which)
        pltpu.make_async_copy(view, view, recv_sems.at[which]).wait()
        own[which].wait()

    for which in range(3):
        arrived(which)

    score_scale = 1.0 / math.sqrt(HEAD_DIM)
    block = max(slab, min(rows, (1 << 18) // tokens))
    blocks = rows // block
    dims = (((1,), (1,)), ((), ()))

    def probs_block(i, carry):
        at = row_slab(i, block)
        q = q_buf[at, :]
        fresh = lax.dot_general(q, kv_buf[0], dims, preferred_element_type=jnp.float32)
        stale = lax.dot_general(q, kv_buf[1], dims, preferred_element_type=jnp.float32)
        fresh_ok = k_rank[0:1, :] <= q_rank[at, 0:1]
        scores = jnp.where(fresh_ok, fresh, stale) * score_scale
        top = jnp.max(scores, axis=1, keepdims=True)
        weights = jnp.exp(scores - top)
        total = jnp.sum(weights, axis=1, keepdims=True)
        probs = weights * (1.0 / total)
        p_fresh[at, :] = jnp.where(fresh_ok, probs, 0.0).astype(jnp.bfloat16)
        p_stale[at, :] = jnp.where(fresh_ok, 0.0, probs).astype(jnp.bfloat16)
        return carry

    lax.fori_loop(0, blocks, probs_block, 0)

    for which in range(3, 5):
        arrived(which)

    per_block = block // slab

    def give_back(i):
        def one(j, carry):
            target = i * per_block + j

            @pl.when(target != me)
            def _():
                pltpu.make_async_remote_copy(
                    src_ref=o_buf.at[row_slab(target, slab), :],
                    dst_ref=out_ref.at[row_slab(my_member, slab), columns(my_head)],
                    send_sem=out_send,
                    recv_sem=out_recv,
                    device_id={"tok": target},
                    device_id_type=MESH,
                ).start()

            return carry

        lax.fori_loop(0, per_block, one, 0)

    def attend_block(i, carry):
        at = row_slab(i, block)
        mixed = jnp.dot(p_fresh[at, :], kv_buf[2], preferred_element_type=jnp.float32)
        mixed = mixed + jnp.dot(p_stale[at, :], kv_buf[3], preferred_element_type=jnp.float32)
        o_buf[at, :] = mixed.astype(jnp.bfloat16)
        give_back(i)
        return carry

    lax.fori_loop(0, blocks, attend_block, 0)
    mine = pltpu.make_async_copy(
        o_buf.at[row_slab(me, slab), :],
        out_ref.at[row_slab(my_member, slab), columns(my_head)],
        own_sem.at[0],
    )
    mine.start()
    for which in range(5):
        view = all_of(which)
        pltpu.make_async_copy(view, view, send_sems.at[which]).wait()
    view = o_buf.at[0 : (devices - 1) * slab, :]
    mine.wait()
    pltpu.make_async_copy(view, view, out_send).wait()
    pltpu.make_async_copy(view, view, out_recv).wait()


def shards(queries, fresh_keys, fresh_values, stale_keys, stale_values, patch_starts, order_starts):
    devices = lax.axis_size("tok")
    tok_dev, width = queries.shape
    slab = tok_dev // (devices // HEADS)
    tokens, rows = devices * tok_dev, devices * slab
    anywhere = pl.BlockSpec(memory_space=pl.ANY)
    scalars = pl.BlockSpec(memory_space=pltpu.SMEM)
    return pl.pallas_call(
        functools.partial(attention_kernel, devices),
        out_shape=jax.ShapeDtypeStruct((tok_dev, width), jnp.bfloat16),
        in_specs=[scalars] * 2 + [anywhere] * 5,
        out_specs=anywhere,
        scratch_shapes=[
            pltpu.VMEM((rows, HEAD_DIM), jnp.bfloat16),
            pltpu.VMEM((4, tokens, HEAD_DIM), jnp.bfloat16),
            pltpu.VMEM((rows, tokens), jnp.bfloat16),
            pltpu.VMEM((rows, tokens), jnp.bfloat16),
            pltpu.VMEM((rows, HEAD_DIM), jnp.bfloat16),
            pltpu.VMEM((rows, HEAD_DIM), jnp.int32),
            pltpu.VMEM((8, tokens), jnp.int32),
            pltpu.SemaphoreType.DMA((5,)),
            pltpu.SemaphoreType.DMA((5,)),
            pltpu.SemaphoreType.DMA((5,)),
            pltpu.SemaphoreType.DMA,
            pltpu.SemaphoreType.DMA,
        ],
        compiler_params=pltpu.CompilerParams(
            collective_id=0, has_side_effects=True, vmem_limit_bytes=60 * 1024 * 1024
        ),
    )(
        patch_starts,
        order_starts,
        queries,
        fresh_keys,
        stale_keys,
        fresh_values,
        stale_values,
    )


def rank_table(patch_starts, order_starts):
    patches = patch_starts.shape[0]
    starts = [patch_starts[p] for p in range(patches)]
    orders = [order_starts[p] for p in range(patches)]
    ranks = []
    for p in range(patches):
        rank = jnp.int32(0)
        for i in range(patches):
            rank = rank + jnp.where(orders[i] == starts[p], jnp.int32(i), jnp.int32(0))
        ranks.append(rank)
    jumps = [ranks[0]] + [ranks[p] - ranks[p - 1] for p in range(1, patches)]

    def rank_at(positions):
        total = jnp.zeros(positions.shape, jnp.int32)
        for p in range(patches):
            total = total + jnp.where(positions >= starts[p], jumps[p], 0)
        return total

    return rank_at


def seat(device, half):
    shift = jnp.where(device >= half, LAYER, 0)
    return lax.rem(lax.rem(device, half) + shift, half)


def is_inner(device, half):
    return seat(device, half) >= LAYER


def halves_kernel(
    devices,
    starts_in,
    orders_in,
    queries,
    fresh_keys,
    stale_keys,
    fresh_values,
    stale_values,
    parts_ref,
    shares_ref,
    q_buf,
    k_buf,
    v_buf,
    p_fresh,
    p_stale,
    o_buf,
    stats,
    shares,
    q_rank,
    k_rank,
    sent,
    q_recv,
    k_recv,
    v_recv,
    o_recv,
    s_send,
    s_recv,
    ready,
    layout,
    layout_sem,
    lse,
    twin_lse,
    twin_part,
    edge_part,
    l_send,
    l_recv,
    t_recv,
):
    me = lax.axis_index("tok")
    tok_dev = queries.shape[0]
    half = devices // 2
    held = HEADS // half
    tokens = devices * tok_dev
    keys = half * tok_dev
    side, place = lax.div(me, half), lax.rem(me, half)
    outer_rows = LAYER * tok_dev
    my_group = seat(me, half)
    inner = my_group >= LAYER
    outer = jnp.logical_not(inner)
    plane = lax.div(me, LAYER)
    other_plane = plane + 1 - 2 * lax.rem(plane, 2)
    outward = jnp.where(side == 0, -LAYER, LAYER)
    twin = me - outward
    near_outer = jnp.where(side == 0, 0, devices - LAYER)
    far_outer = devices - LAYER - near_outer
    barrier = pltpu.get_barrier_semaphore()

    def near_peer(step):
        return side * half + lax.rem(place + step, half)

    def far_peer(step):
        return (1 - side) * half + lax.rem(place + step, half)

    def columns(head):
        return pl.ds(pl.multiple_of(head * HEAD_DIM, HEAD_DIM), HEAD_DIM)

    def row_slab(index, size, count=1):
        return pl.ds(pl.multiple_of(index * size, size), size * count)

    def signal(sem, device):
        pl.semaphore_signal(sem, inc=1, device_id={"tok": device}, device_id_type=MESH)

    def greet(step, carry):
        signal(barrier, near_peer(step))
        return carry

    @pl.when(inner)
    def _():
        signal(barrier, twin)

    lax.fori_loop(1, half, greet, 0)
    layout_copies = [
        pltpu.make_async_copy(whole, layout.at[n], layout_sem.at[n])
        for n, whole in enumerate((starts_in, orders_in))
    ]
    for copy in layout_copies:
        copy.start()

    def send(src, dst, send_sem, recv_sem, device):
        pltpu.make_async_remote_copy(
            src_ref=src,
            dst_ref=dst,
            send_sem=send_sem,
            recv_sem=recv_sem,
            device_id={"tok": device},
            device_id_type=MESH,
        ).start()

    sources = {"Q": (queries,), "K": (fresh_keys, stale_keys), "V": (fresh_values, stale_values)}
    def landed(kind, head):
        if kind == "Q":
            return q_recv.at[head, plane]
        return (k_recv if kind == "K" else v_recv).at[head]


    def landing(kind, head, which):
        if kind == "Q":
            return q_buf.at[head, row_slab(me, tok_dev), :]
        return (k_buf if kind == "K" else v_buf).at[head, which, row_slab(place, tok_dev), :]

    def source(kind, head, which, device):
        return sources[kind][which].at[:, columns(head * half + seat(device, half))]

    def share_out(kind, head, spread):
        def go(step, peer):
            for which in range(len(sources[kind])):
                send(
                    source(kind, head, which, peer),
                    landing(kind, head, which),
                    sent,
                    landed(kind, head),
                    peer,
                )

        def cross(step, carry):
            go(step, other_plane * LAYER + lax.rem(me + step, LAYER))
            return carry

        def beside(step, carry):
            go(step, plane * LAYER + lax.rem(me + step, LAYER))
            return carry

        def far(step, carry):
            peer = far_peer(step)
            pl.when(jnp.logical_or(inner, jnp.logical_not(is_inner(peer, half))))(
                lambda: go(step, peer)
            )
            return carry

        if "cross" in spread:
            lax.fori_loop(0, LAYER, cross, 0)
        if "beside" in spread:
            lax.fori_loop(1, LAYER, beside, 0)
        if "far" in spread:
            lax.fori_loop(0, half, far, 0)

    def pass_on(head):
        @pl.when(inner)
        def _():
            view = q_buf.at[head, row_slab(near_outer, tok_dev, LAYER), :]
            pltpu.make_async_copy(view, view, q_recv.at[head, other_plane]).wait()
            send(view, view, sent, q_recv.at[head, other_plane], twin)

    def start_all(steps):
        for kind, head, spread, who in steps:
            if kind == "pass":
                pass_on(head)
            elif kind == "ready":
                pl.semaphore_wait(ready, 1)

                @pl.when(inner)
                def _():
                    signal(ready, me + outward)

            elif who is not None:
                pl.when(inner if who == "inner" else outer)(
                    lambda kind=kind, head=head, spread=spread: share_out(kind, head, spread)
                )
            else:
                share_out(kind, head, spread)

    pl.semaphore_wait(barrier, half - 1 + inner.astype(jnp.int32))

    @pl.when(inner)
    def _():
        signal(ready, twin)

    start_all(ISSUE[0])

    for head in range(held):
        for kind in "QKV":
            for which in range(len(sources[kind])):
                pltpu.make_async_copy(
                    source(kind, head, which, me), landing(kind, head, which), landed(kind, head)
                ).start()

    for copy in layout_copies:
        copy.wait()
    rank_at = rank_table(layout.at[0], layout.at[1])
    k_rank[...] = rank_at(keys * side + lax.broadcasted_iota(jnp.int32, k_rank.shape, 1))

    def fill_rank(device, carry):
        q_rank[row_slab(device, tok_dev), :] = rank_at(
            device * tok_dev + lax.broadcasted_iota(jnp.int32, (tok_dev, HEAD_DIM), 0)
        )
        return carry

    lax.fori_loop(0, devices, fill_rank, 0)

    def whole_wait(view, sem):
        pltpu.make_async_copy(view, view, sem).wait()

    def arrived(kind, head):
        whole_wait((k_buf if kind == "K" else v_buf).at[head], landed(kind, head))

    def asked(head, i):
        @pl.when(jnp.logical_not(jnp.logical_and(inner, i == other_plane)))
        def _():
            whole_wait(q_buf.at[head, row_slab(i, outer_rows), :], q_recv.at[head, i])

    score_scale = 1.0 / math.sqrt(HEAD_DIM)
    block = outer_rows
    dims = (((1,), (1,)), ((), ()))
    owner_tile = 128 // tok_dev
    edge_tiles = outer_rows // 128

    def plane_order(n):
        last = devices // LAYER - 1
        swapped = jnp.where(n >= 2, 5 - n, n)
        return jnp.where(side == 0, last - swapped, swapped)

    def send_levels(head, i):
        def one(j, carry):
            target = i * LAYER + j

            @pl.when(target != me)
            def _():
                src = lse.at[head, lax.div(target, owner_tile)]
                send(src, stats.at[head, me], s_send, s_recv.at[head], target)

            return carry

        lax.fori_loop(0, LAYER, one, 0)

        @pl.when(jnp.logical_and(inner, i * LAYER == far_outer))
        def _():
            src = lse.at[head, pl.ds(far_outer // owner_tile, edge_tiles)]
            send(src, twin_lse.at[head], l_send, l_recv.at[head], twin)

    def hand_out(head, target):
        send(
            o_buf.at[head, row_slab(target, tok_dev), :],
            parts_ref.at[side, :, columns(head * half + my_group)],
            sent,
            o_recv.at[head],
            target,
        )

    def join(head):
        @pl.when(inner)
        def _():
            whole_wait(twin_lse.at[head], l_recv.at[head])
            whole_wait(twin_part.at[head], t_recv.at[head])
            for tile in range(edge_tiles):
                mine, theirs = lse[head, near_outer // owner_tile + tile], twin_lse[head, tile]
                w_mine = jnp.broadcast_to(1.0 / (1.0 + jnp.exp(theirs - mine)), (128, 128))
                w_theirs = jnp.broadcast_to(1.0 / (1.0 + jnp.exp(mine - theirs)), (128, 128))
                spot = slice(tile * 128, (tile + 1) * 128)
                full = edge_part[head, spot, :] * jnp.transpose(w_mine)
                full = full + twin_part[head, spot, :].astype(jnp.float32) * jnp.transpose(w_theirs)
                at = pl.ds(pl.multiple_of(near_outer * tok_dev + tile * 128, 128), 128)
                o_buf[head, at, :] = full.astype(jnp.bfloat16)

            def one(j, carry):
                hand_out(head, near_outer + j)
                return carry

            lax.fori_loop(0, LAYER, one, 0)


    for head in range(held):
        arrived("K", head)
        start_all(ISSUE[1 + 3 * head])

        def probs_block(n, carry, head=head):
            i = plane_order(n)
            asked(head, i)
            at = row_slab(i, block)
            q = q_buf[head, at, :]
            fresh = lax.dot_general(q, k_buf[head, 0], dims, preferred_element_type=jnp.float32)
            stale = lax.dot_general(q, k_buf[head, 1], dims, preferred_element_type=jnp.float32)
            fresh_ok = k_rank[0:1, :] <= q_rank[at, 0:1]
            scores = jnp.where(fresh_ok, fresh, stale) * score_scale
            top = jnp.max(scores, axis=1, keepdims=True)
            weights = jnp.exp(scores - top)
            total = jnp.sum(weights, axis=1, keepdims=True)
            probs = weights * (1.0 / total)
            p_fresh[head, at, :] = jnp.where(fresh_ok, probs, 0.0).astype(jnp.bfloat16)
            p_stale[head, at, :] = jnp.where(fresh_ok, 0.0, probs).astype(jnp.bfloat16)
            level = jnp.broadcast_to(top + jnp.log(total), (block, 128))
            for tile in range(block // 128):
                turned = jnp.transpose(level[tile * 128 : (tile + 1) * 128, :])
                lse[head, i * (block // 128) + tile] = turned[0:1, :]
            send_levels(head, i)
            return carry

        def attend_block(n, carry, head=head):
            i = plane_order(n)
            at = row_slab(i, outer_rows)
            mixed = jnp.dot(p_fresh[head, at, :], v_buf[head, 0], preferred_element_type=jnp.float32)
            mixed = mixed + jnp.dot(
                p_stale[head, at, :], v_buf[head, 1], preferred_element_type=jnp.float32
            )
            o_buf[head, at, :] = mixed.astype(jnp.bfloat16)

            @pl.when(jnp.logical_and(inner, i * LAYER == near_outer))
            def _():
                edge_part[head] = mixed

            @pl.when(jnp.logical_and(inner, i * LAYER == far_outer))
            def _():
                src = o_buf.at[head, row_slab(far_outer, tok_dev, LAYER), :]
                send(src, twin_part.at[head], sent, t_recv.at[head], twin)

            def give_back(j, carry):
                target = i * LAYER + j
                direct = jnp.logical_or(outer, is_inner(target, half))

                @pl.when(jnp.logical_and(target != me, direct))
                def _():
                    hand_out(head, target)

                return carry

            lax.fori_loop(0, LAYER, give_back, 0)
            return carry

        planes = devices // LAYER
        early = planes - HELD_BACK[head]
        lax.fori_loop(0, early, probs_block, 0)
        start_all(ISSUE[2 + 3 * head])
        arrived("V", head)
        start_all(ISSUE[3 + 3 * head])
        lax.fori_loop(0, early, attend_block, 0)
        if head > 0:
            join(head - 1)
        if early < planes:
            lax.fori_loop(early, planes, probs_block, 0)
            lax.fori_loop(early, planes, attend_block, 0)

    join(held - 1)
    for head in range(held):
        pltpu.make_async_copy(
            o_buf.at[head, row_slab(me, tok_dev), :],
            parts_ref.at[side, :, columns(head * half + my_group)],
            o_recv.at[head],
        ).start()
        pltpu.make_async_copy(
            lse.at[head, lax.div(me, owner_tile)], stats.at[head, me], s_recv.at[head]
        ).start()

    def outputs_in(head):
        @pl.when(inner)
        def _():
            whole_wait(o_buf.at[head], o_recv.at[head])

        @pl.when(outer)
        def _():
            whole_wait(o_buf.at[head, 0 : (devices - LAYER) * tok_dev, :], o_recv.at[head])

    for head in range(held):
        whole_wait(stats.at[head], s_recv.at[head])

        def levels(of_side, head=head):
            return jnp.concatenate(
                [
                    stats[head, of_side * half + (group + of_side * LAYER) % half]
                    for group in range(half)
                ],
                axis=0,
            )

        share = 1.0 / (1.0 + jnp.exp(levels(1) - levels(0)))
        share = jnp.concatenate([share, jnp.zeros((128 - half, 128), jnp.float32)], axis=0)
        shares[...] = jnp.transpose(share)
        rows = row_slab(lax.rem(me, owner_tile), tok_dev)
        if head < held - 1:
            outputs_in(head)
            merge_slot(head, half, parts_ref, shares.at[rows, :], outer, side, parts_ref.at[0])
        else:
            shares_ref[...] = shares[rows, :]

    outputs_in(held - 1)
    whole_wait(stats.at[:, 0 : devices - 1], s_send)
    slab = tok_dev * HEAD_DIM

    def all_sent(slabs):
        whole_wait(p_fresh.at[:, 0 : slabs * slab // keys, :], sent)

    kv, out = 4 * (half - 1), devices - 1

    @pl.when(inner)
    def _():
        whole_wait(twin_lse, l_send)
        all_sent(kv + devices - 1 + LAYER + out)

    @pl.when(outer)
    def _():
        all_sent(kv + devices - 1 - LAYER + out)


def merge_slot(slot, half, parts, shares, outer, side, out):
    for head in range(slot * half, (slot + 1) * half):
        at = slice(head * HEAD_DIM, (head + 1) * HEAD_DIM)

        def both(at=at, head=head):
            low, high = parts[0, :, at].astype(jnp.float32), parts[1, :, at].astype(jnp.float32)
            share = shares[:, head % half : head % half + 1]
            out[:, at] = (high + (low - high) * share).astype(jnp.bfloat16)

        if head % half < LAYER:
            both()
        else:
            pl.when(jnp.logical_not(outer))(both)

            @pl.when(outer)
            def _(at=at):
                out[:, at] = parts[side, :, at]


def merge_kernel(devices, parts, shares, out_ref, merged, out_sems):
    half = devices // 2
    me = lax.axis_index("tok")
    last = HEADS // half - 1
    done = last * half * HEAD_DIM
    early = pltpu.make_async_copy(
        parts.at[0, :, 0:done], out_ref.at[:, 0:done], out_sems.at[0]
    )
    early.start()
    outer = jnp.logical_not(is_inner(me, half))
    merge_slot(last, half, parts, shares, outer, lax.div(me, half), merged)
    late = pltpu.make_async_copy(merged.at[:, done:], out_ref.at[:, done:], out_sems.at[1])
    late.start()
    early.wait()
    late.wait()


def halves(*arrays):
    arrays = [pltpu.with_memory_space_constraint(array, pltpu.HBM) for array in arrays]
    queries, fresh_keys, fresh_values, stale_keys, stale_values, patch_starts, order_starts = arrays
    devices = lax.axis_size("tok")
    tok_dev, width = queries.shape
    half = devices // 2
    held = HEADS // half
    tokens, keys = devices * tok_dev, half * tok_dev
    anywhere = pl.BlockSpec(memory_space=pl.ANY)
    main_memory = pl.BlockSpec(memory_space=pltpu.HBM)
    near_memory = pl.BlockSpec(memory_space=pltpu.VMEM)
    patches = patch_starts.shape[0]
    dma = pltpu.SemaphoreType.DMA
    parts, shares = pl.pallas_call(
        functools.partial(halves_kernel, devices),
        out_shape=(
            jax.ShapeDtypeStruct((2, tok_dev, width), jnp.bfloat16),
            jax.ShapeDtypeStruct((tok_dev, 128), jnp.float32),
        ),
        in_specs=[main_memory] * 7,
        out_specs=(near_memory, near_memory),
        scratch_shapes=[
            pltpu.VMEM((held, tokens, HEAD_DIM), jnp.bfloat16),
            pltpu.VMEM((held, 2, keys, HEAD_DIM), jnp.bfloat16),
            pltpu.VMEM((held, 2, keys, HEAD_DIM), jnp.bfloat16),
            pltpu.VMEM((held, tokens, keys), jnp.bfloat16),
            pltpu.VMEM((held, tokens, keys), jnp.bfloat16),
            pltpu.VMEM((held, tokens, HEAD_DIM), jnp.bfloat16),
            pltpu.VMEM((held, devices, 1, 128), jnp.float32),
            pltpu.VMEM((128, 128), jnp.float32),
            pltpu.VMEM((tokens, HEAD_DIM), jnp.int32),
            pltpu.VMEM((8, keys), jnp.int32),
            dma,
            dma((held, devices // LAYER)),
            dma((held,)),
            dma((held,)),
            dma((held,)),
            dma,
            dma((held,)),
            pltpu.SemaphoreType.REGULAR,
            pltpu.SMEM((2, patches), jnp.int32),
            dma((2,)),
            pltpu.VMEM((held, tokens // 128, 1, 128), jnp.float32),
            pltpu.VMEM((held, LAYER * tok_dev // 128, 1, 128), jnp.float32),
            pltpu.VMEM((held, LAYER * tok_dev, HEAD_DIM), jnp.bfloat16),
            pltpu.VMEM((held, LAYER * tok_dev, HEAD_DIM), jnp.float32),
            dma,
            dma((held,)),
            dma((held,)),
        ],
        compiler_params=pltpu.CompilerParams(
            collective_id=0, has_side_effects=True, vmem_limit_bytes=32 * 1024 * 1024
        ),
    )(patch_starts, order_starts, queries, fresh_keys, stale_keys, fresh_values, stale_values)
    return pl.pallas_call(
        functools.partial(merge_kernel, devices),
        out_shape=jax.ShapeDtypeStruct((tok_dev, width), jnp.bfloat16),
        in_specs=[near_memory, near_memory],
        out_specs=main_memory,
        scratch_shapes=[pltpu.VMEM((tok_dev, width), jnp.bfloat16), dma((2,))],
        compiler_params=pltpu.CompilerParams(vmem_limit_bytes=16 * 1024 * 1024),
    )(parts, shares)


def solution(mesh):
    placed = (P(("groups", "tok"), None),) * 5 + (P("groups"),) * 2
    devices = mesh.shape["tok"]

    def body(*arrays):
        tok_dev = arrays[0].shape[0]
        split = devices % 2 == 0 and HEADS % (devices // 2) == 0
        split = split and devices // 2 == 2 * LAYER and LAYER * tok_dev % 128 == 0
        split = split and 2 * LAYER * tok_dev == 512
        split = split and 128 % tok_dev == 0 and devices * tok_dev % 512 == 0
        return (halves if split else shards)(*arrays)

    return jax.shard_map(
        body, mesh=mesh, in_specs=placed, out_specs=P(("groups", "tok"), None), check_vma=False
    )
```

```python
import functools
import math

import jax
import jax.numpy as jnp
from jax import lax
from jax.experimental import pallas as pl
from jax.experimental.pallas import tpu as pltpu
from jax.sharding import PartitionSpec as P

HEADS = 16
HEAD_DIM = 128
LAYER = 4
ISSUE = ((('Q', 0, ('straight',), None), ('K', 0, ('straight',), None), ('Q', 0, ('beside',), None), ('wide', 0, (), None), ('Q', 0, ('diagonal',), None), ('K', 0, ('diagonal',), None), ('K', 0, ('beside',), None), ('ready', 0, (), None), ('Q', 0, ('far',), None), ('V', 0, ('straight', 'beside', 'diagonal'), None), ('Q', 1, ('straight', 'diagonal'), 'outer'), ('Q', 1, ('beside',), None), ('pass', 0, (), None), ('Q', 1, ('far',), None), ('K', 1, ('straight', 'beside', 'diagonal'), None), ('V', 1, ('straight', 'beside', 'diagonal'), None)), (), (('pass', 1, (), None), ('Q', 1, ('straight', 'diagonal'), 'inner')), (), (), (), ())
HELD_BACK = (0, 1)
MESH = pl.DeviceIdType.MESH


def attention_kernel(
    devices,
    patch_starts,
    order_starts,
    queries,
    fresh_keys,
    stale_keys,
    fresh_values,
    stale_values,
    out_ref,
    q_buf,
    kv_buf,
    p_fresh,
    p_stale,
    o_buf,
    q_rank,
    k_rank,
    send_sems,
    recv_sems,
    own_sem,
    out_send,
    out_recv,
):
    me = lax.axis_index("tok")
    tok_dev = queries.shape[0]
    group_size = devices // HEADS
    slab = tok_dev // group_size
    tokens = devices * tok_dev
    rows = devices * slab
    my_head = me // group_size
    my_member = me % group_size
    barrier = pltpu.get_barrier_semaphore()

    def peer_of(step):
        return lax.rem(me + step, devices)

    def columns(head):
        return pl.ds(pl.multiple_of(head * HEAD_DIM, HEAD_DIM), HEAD_DIM)

    def row_slab(index, size):
        return pl.ds(pl.multiple_of(index * size, size), size)

    def greet(step, carry):
        pl.semaphore_signal(barrier, inc=1, device_id={"tok": peer_of(step)}, device_id_type=MESH)
        return carry

    lax.fori_loop(1, devices, greet, 0)

    sources = (queries, fresh_keys, stale_keys, fresh_values, stale_values)

    def source_view(which, device):
        head, member = device // group_size, device % group_size
        if which == 0:
            return queries.at[row_slab(member, slab), columns(head)]
        return sources[which].at[:, columns(head)]

    def landing(which, device):
        if which == 0:
            return q_buf.at[row_slab(device, slab), :]
        return kv_buf.at[which - 1, row_slab(device, tok_dev), :]

    own = [
        pltpu.make_async_copy(source_view(which, me), landing(which, me), own_sem.at[which])
        for which in range(5)
    ]
    for copy in own:
        copy.start()
    pl.semaphore_wait(barrier, devices - 1)

    for which in range(5):

        def send(step, carry, which=which):
            peer = peer_of(step)
            pltpu.make_async_remote_copy(
                src_ref=source_view(which, peer),
                dst_ref=landing(which, me),
                send_sem=send_sems.at[which],
                recv_sem=recv_sems.at[which],
                device_id={"tok": peer},
                device_id_type=MESH,
            ).start()
            return carry

        lax.fori_loop(1, devices, send, 0)

    patches = patch_starts.shape[0]
    starts = [patch_starts[p] for p in range(patches)]
    orders = [order_starts[p] for p in range(patches)]
    ranks = []
    for p in range(patches):
        rank = jnp.int32(0)
        for i in range(patches):
            rank = rank + jnp.where(orders[i] == starts[p], jnp.int32(i), jnp.int32(0))
        ranks.append(rank)
    jumps = [ranks[0]] + [ranks[p] - ranks[p - 1] for p in range(1, patches)]

    def rank_at(positions):
        total = jnp.zeros(positions.shape, jnp.int32)
        for p in range(patches):
            total = total + jnp.where(positions >= starts[p], jumps[p], 0)
        return total

    k_rank[...] = rank_at(lax.broadcasted_iota(jnp.int32, k_rank.shape, 1))

    def fill_rank(device, carry):
        base = device * tok_dev + my_member * slab
        q_rank[row_slab(device, slab), :] = rank_at(
            base + lax.broadcasted_iota(jnp.int32, (slab, HEAD_DIM), 0)
        )
        return carry

    lax.fori_loop(0, devices, fill_rank, 0)

    def all_of(which):
        size = (devices - 1) * (slab if which == 0 else tok_dev)
        return q_buf.at[0:size, :] if which == 0 else kv_buf.at[which - 1, 0:size, :]

    def arrived(which):
        view = all_of(which)
        pltpu.make_async_copy(view, view, recv_sems.at[which]).wait()
        own[which].wait()

    for which in range(3):
        arrived(which)

    score_scale = 1.0 / math.sqrt(HEAD_DIM)
    block = max(slab, min(rows, (1 << 18) // tokens))
    blocks = rows // block
    dims = (((1,), (1,)), ((), ()))

    def probs_block(i, carry):
        at = row_slab(i, block)
        q = q_buf[at, :]
        fresh = lax.dot_general(q, kv_buf[0], dims, preferred_element_type=jnp.float32)
        stale = lax.dot_general(q, kv_buf[1], dims, preferred_element_type=jnp.float32)
        fresh_ok = k_rank[0:1, :] <= q_rank[at, 0:1]
        scores = jnp.where(fresh_ok, fresh, stale) * score_scale
        top = jnp.max(scores, axis=1, keepdims=True)
        weights = jnp.exp(scores - top)
        total = jnp.sum(weights, axis=1, keepdims=True)
        probs = weights * (1.0 / total)
        p_fresh[at, :] = jnp.where(fresh_ok, probs, 0.0).astype(jnp.bfloat16)
        p_stale[at, :] = jnp.where(fresh_ok, 0.0, probs).astype(jnp.bfloat16)
        return carry

    lax.fori_loop(0, blocks, probs_block, 0)

    for which in range(3, 5):
        arrived(which)

    per_block = block // slab

    def give_back(i):
        def one(j, carry):
            target = i * per_block + j

            @pl.when(target != me)
            def _():
                pltpu.make_async_remote_copy(
                    src_ref=o_buf.at[row_slab(target, slab), :],
                    dst_ref=out_ref.at[row_slab(my_member, slab), columns(my_head)],
                    send_sem=out_send,
                    recv_sem=out_recv,
                    device_id={"tok": target},
                    device_id_type=MESH,
                ).start()

            return carry

        lax.fori_loop(0, per_block, one, 0)

    def attend_block(i, carry):
        at = row_slab(i, block)
        mixed = jnp.dot(p_fresh[at, :], kv_buf[2], preferred_element_type=jnp.float32)
        mixed = mixed + jnp.dot(p_stale[at, :], kv_buf[3], preferred_element_type=jnp.float32)
        o_buf[at, :] = mixed.astype(jnp.bfloat16)
        give_back(i)
        return carry

    lax.fori_loop(0, blocks, attend_block, 0)
    mine = pltpu.make_async_copy(
        o_buf.at[row_slab(me, slab), :],
        out_ref.at[row_slab(my_member, slab), columns(my_head)],
        own_sem.at[0],
    )
    mine.start()
    for which in range(5):
        view = all_of(which)
        pltpu.make_async_copy(view, view, send_sems.at[which]).wait()
    view = o_buf.at[0 : (devices - 1) * slab, :]
    mine.wait()
    pltpu.make_async_copy(view, view, out_send).wait()
    pltpu.make_async_copy(view, view, out_recv).wait()


def shards(queries, fresh_keys, fresh_values, stale_keys, stale_values, patch_starts, order_starts):
    devices = lax.axis_size("tok")
    tok_dev, width = queries.shape
    slab = tok_dev // (devices // HEADS)
    tokens, rows = devices * tok_dev, devices * slab
    anywhere = pl.BlockSpec(memory_space=pl.ANY)
    scalars = pl.BlockSpec(memory_space=pltpu.SMEM)
    return pl.pallas_call(
        functools.partial(attention_kernel, devices),
        out_shape=jax.ShapeDtypeStruct((tok_dev, width), jnp.bfloat16),
        in_specs=[scalars] * 2 + [anywhere] * 5,
        out_specs=anywhere,
        scratch_shapes=[
            pltpu.VMEM((rows, HEAD_DIM), jnp.bfloat16),
            pltpu.VMEM((4, tokens, HEAD_DIM), jnp.bfloat16),
            pltpu.VMEM((rows, tokens), jnp.bfloat16),
            pltpu.VMEM((rows, tokens), jnp.bfloat16),
            pltpu.VMEM((rows, HEAD_DIM), jnp.bfloat16),
            pltpu.VMEM((rows, HEAD_DIM), jnp.int32),
            pltpu.VMEM((8, tokens), jnp.int32),
            pltpu.SemaphoreType.DMA((5,)),
            pltpu.SemaphoreType.DMA((5,)),
            pltpu.SemaphoreType.DMA((5,)),
            pltpu.SemaphoreType.DMA,
            pltpu.SemaphoreType.DMA,
        ],
        compiler_params=pltpu.CompilerParams(
            collective_id=0, has_side_effects=True, vmem_limit_bytes=60 * 1024 * 1024
        ),
    )(
        patch_starts,
        order_starts,
        queries,
        fresh_keys,
        stale_keys,
        fresh_values,
        stale_values,
    )


def rank_table(patch_starts, order_starts):
    patches = patch_starts.shape[0]
    starts = [patch_starts[p] for p in range(patches)]
    orders = [order_starts[p] for p in range(patches)]
    ranks = []
    for p in range(patches):
        rank = jnp.int32(0)
        for i in range(patches):
            rank = rank + jnp.where(orders[i] == starts[p], jnp.int32(i), jnp.int32(0))
        ranks.append(rank)
    jumps = [ranks[0]] + [ranks[p] - ranks[p - 1] for p in range(1, patches)]

    def rank_at(positions):
        total = jnp.zeros(positions.shape, jnp.int32)
        for p in range(patches):
            total = total + jnp.where(positions >= starts[p], jumps[p], 0)
        return total

    return rank_at


def seat(device, half):
    shift = jnp.where(device >= half, LAYER, 0)
    return lax.rem(lax.rem(device, half) + shift, half)


def is_inner(device, half):
    return seat(device, half) >= LAYER


def halves_kernel(
    devices,
    starts_in,
    orders_in,
    queries,
    fresh_keys,
    stale_keys,
    fresh_values,
    stale_values,
    parts_ref,
    shares_ref,
    q_buf,
    k_buf,
    v_buf,
    p_fresh,
    p_stale,
    o_buf,
    stats,
    shares,
    q_rank,
    k_rank,
    sent,
    q_recv,
    k_recv,
    v_recv,
    o_recv,
    s_send,
    s_recv,
    ready,
    wide,
    layout,
    layout_sem,
    lse,
    twin_lse,
    twin_part,
    edge_part,
    l_send,
    l_recv,
    t_recv,
):
    me = lax.axis_index("tok")
    tok_dev = queries.shape[0]
    half = devices // 2
    held = HEADS // half
    tokens = devices * tok_dev
    keys = half * tok_dev
    side, place = lax.div(me, half), lax.rem(me, half)
    outer_rows = LAYER * tok_dev
    my_group = seat(me, half)
    inner = my_group >= LAYER
    outer = jnp.logical_not(inner)
    plane = lax.div(me, LAYER)
    other_plane = plane + 1 - 2 * lax.rem(plane, 2)
    outward = jnp.where(side == 0, -LAYER, LAYER)
    twin = me - outward
    near_outer = jnp.where(side == 0, 0, devices - LAYER)
    far_outer = devices - LAYER - near_outer
    barrier = pltpu.get_barrier_semaphore()

    column = lax.rem(me, LAYER)
    mirror = me + 2 - LAYER * lax.div(column, 2)

    def straight_peer(step):
        return other_plane * LAYER + 2 * lax.div(column, 2) + step

    def diagonal_peer(step):
        return other_plane * LAYER + 2 - 2 * lax.div(column, 2) + step

    def far_peer(step):
        return (1 - side) * half + lax.rem(place + step, half)

    def columns(head):
        return pl.ds(pl.multiple_of(head * HEAD_DIM, HEAD_DIM), HEAD_DIM)

    def row_slab(index, size, count=1):
        return pl.ds(pl.multiple_of(index * size, size), size * count)

    def signal(sem, device):
        pl.semaphore_signal(sem, inc=1, device_id={"tok": device}, device_id_type=MESH)


    @pl.when(inner)
    def _():
        signal(barrier, twin)

    for step in range(1, LAYER):
        signal(barrier, plane * LAYER + lax.rem(me + step, LAYER))
    for step in range(2):
        signal(barrier, straight_peer(step))
    layout_copies = [
        pltpu.make_async_copy(whole, layout.at[n], layout_sem.at[n])
        for n, whole in enumerate((starts_in, orders_in))
    ]
    for copy in layout_copies:
        copy.start()

    def send(src, dst, send_sem, recv_sem, device):
        pltpu.make_async_remote_copy(
            src_ref=src,
            dst_ref=dst,
            send_sem=send_sem,
            recv_sem=recv_sem,
            device_id={"tok": device},
            device_id_type=MESH,
        ).start()

    sources = {"Q": (queries,), "K": (fresh_keys, stale_keys), "V": (fresh_values, stale_values)}
    def landed(kind, head):
        if kind == "Q":
            return q_recv.at[head, plane]
        return (k_recv if kind == "K" else v_recv).at[head]


    def landing(kind, head, which):
        if kind == "Q":
            return q_buf.at[head, row_slab(me, tok_dev), :]
        return (k_buf if kind == "K" else v_buf).at[head, which, row_slab(place, tok_dev), :]

    def source(kind, head, which, device):
        return sources[kind][which].at[:, columns(head * half + seat(device, half))]

    def share_out(kind, head, spread):
        def go(step, peer):
            for which in range(len(sources[kind])):
                send(
                    source(kind, head, which, peer),
                    landing(kind, head, which),
                    sent,
                    landed(kind, head),
                    peer,
                )

        def straight(step, carry):
            go(step, straight_peer(step))
            return carry

        def diagonal(step, carry):
            go(step, diagonal_peer(step))
            return carry

        def beside(step, carry):
            go(step, plane * LAYER + lax.rem(me + step, LAYER))
            return carry

        def far(step, carry):
            peer = far_peer(step)
            pl.when(jnp.logical_or(inner, jnp.logical_not(is_inner(peer, half))))(
                lambda: go(step, peer)
            )
            return carry

        if "straight" in spread:
            lax.fori_loop(0, 2, straight, 0)
        if "beside" in spread:
            lax.fori_loop(1, LAYER, beside, 0)
        if "diagonal" in spread:
            lax.fori_loop(0, 2, diagonal, 0)
        if "far" in spread:
            lax.fori_loop(0, half, far, 0)

    def pass_on(head):
        @pl.when(inner)
        def _():
            view = q_buf.at[head, row_slab(near_outer, tok_dev, LAYER), :]
            pltpu.make_async_copy(view, view, q_recv.at[head, other_plane]).wait()
            send(view, view, sent, q_recv.at[head, other_plane], twin)

    def start_all(steps):
        for kind, head, spread, who in steps:
            if kind == "pass":
                pass_on(head)
            elif kind == "wide":
                pl.semaphore_wait(wide, 1)

                @pl.when(inner)
                def _():
                    signal(ready, twin)

            elif kind == "ready":
                pl.semaphore_wait(ready, 1)

                @pl.when(inner)
                def _():
                    signal(ready, me + outward)

            elif who is not None:
                pl.when(inner if who == "inner" else outer)(
                    lambda kind=kind, head=head, spread=spread: share_out(kind, head, spread)
                )
            else:
                share_out(kind, head, spread)

    pl.semaphore_wait(barrier, LAYER + 1 + inner.astype(jnp.int32))

    signal(wide, mirror)

    start_all(ISSUE[0])

    for head in range(held):
        for kind in "QKV":
            for which in range(len(sources[kind])):
                pltpu.make_async_copy(
                    source(kind, head, which, me), landing(kind, head, which), landed(kind, head)
                ).start()

    for copy in layout_copies:
        copy.wait()
    rank_at = rank_table(layout.at[0], layout.at[1])
    k_rank[...] = rank_at(keys * side + lax.broadcasted_iota(jnp.int32, k_rank.shape, 1))

    def fill_rank(device, carry):
        q_rank[row_slab(device, tok_dev), :] = rank_at(
            device * tok_dev + lax.broadcasted_iota(jnp.int32, (tok_dev, HEAD_DIM), 0)
        )
        return carry

    lax.fori_loop(0, devices, fill_rank, 0)

    def whole_wait(view, sem):
        pltpu.make_async_copy(view, view, sem).wait()

    def arrived(kind, head):
        whole_wait((k_buf if kind == "K" else v_buf).at[head], landed(kind, head))

    def asked(head, i):
        @pl.when(jnp.logical_not(jnp.logical_and(inner, i == other_plane)))
        def _():
            whole_wait(q_buf.at[head, row_slab(i, outer_rows), :], q_recv.at[head, i])

    score_scale = 1.0 / math.sqrt(HEAD_DIM)
    block = outer_rows
    dims = (((1,), (1,)), ((), ()))
    owner_tile = 128 // tok_dev
    edge_tiles = outer_rows // 128

    def plane_order(n):
        last = devices // LAYER - 1
        swapped = jnp.where(n >= 2, 5 - n, n)
        return jnp.where(side == 0, last - swapped, swapped)

    def send_levels(head, i):
        def one(j, carry):
            target = i * LAYER + j

            @pl.when(target != me)
            def _():
                src = lse.at[head, lax.div(target, owner_tile)]
                send(src, stats.at[head, me], s_send, s_recv.at[head], target)

            return carry

        lax.fori_loop(0, LAYER, one, 0)

        @pl.when(jnp.logical_and(inner, i * LAYER == far_outer))
        def _():
            src = lse.at[head, pl.ds(far_outer // owner_tile, edge_tiles)]
            send(src, twin_lse.at[head], l_send, l_recv.at[head], twin)

    def hand_out(head, target):
        send(
            o_buf.at[head, row_slab(target, tok_dev), :],
            parts_ref.at[side, :, columns(head * half + my_group)],
            sent,
            o_recv.at[head],
            target,
        )

    def join(head):
        @pl.when(inner)
        def _():
            whole_wait(twin_lse.at[head], l_recv.at[head])
            whole_wait(twin_part.at[head], t_recv.at[head])
            for tile in range(edge_tiles):
                mine, theirs = lse[head, near_outer // owner_tile + tile], twin_lse[head, tile]
                w_mine = jnp.broadcast_to(1.0 / (1.0 + jnp.exp(theirs - mine)), (128, 128))
                w_theirs = jnp.broadcast_to(1.0 / (1.0 + jnp.exp(mine - theirs)), (128, 128))
                spot = slice(tile * 128, (tile + 1) * 128)
                full = edge_part[head, spot, :] * jnp.transpose(w_mine)
                full = full + twin_part[head, spot, :].astype(jnp.float32) * jnp.transpose(w_theirs)
                at = pl.ds(pl.multiple_of(near_outer * tok_dev + tile * 128, 128), 128)
                o_buf[head, at, :] = full.astype(jnp.bfloat16)

            def one(j, carry):
                hand_out(head, near_outer + j)
                return carry

            lax.fori_loop(0, LAYER, one, 0)


    for head in range(held):
        arrived("K", head)
        start_all(ISSUE[1 + 3 * head])

        def probs_block(n, carry, head=head):
            i = plane_order(n)
            asked(head, i)
            at = row_slab(i, block)
            q = q_buf[head, at, :]
            fresh = lax.dot_general(q, k_buf[head, 0], dims, preferred_element_type=jnp.float32)
            stale = lax.dot_general(q, k_buf[head, 1], dims, preferred_element_type=jnp.float32)
            fresh_ok = k_rank[0:1, :] <= q_rank[at, 0:1]
            scores = jnp.where(fresh_ok, fresh, stale) * score_scale
            top = jnp.max(scores, axis=1, keepdims=True)
            weights = jnp.exp(scores - top)
            total = jnp.sum(weights, axis=1, keepdims=True)
            probs = weights * (1.0 / total)
            p_fresh[head, at, :] = jnp.where(fresh_ok, probs, 0.0).astype(jnp.bfloat16)
            p_stale[head, at, :] = jnp.where(fresh_ok, 0.0, probs).astype(jnp.bfloat16)
            level = jnp.broadcast_to(top + jnp.log(total), (block, 128))
            for tile in range(block // 128):
                turned = jnp.transpose(level[tile * 128 : (tile + 1) * 128, :])
                lse[head, i * (block // 128) + tile] = turned[0:1, :]
            send_levels(head, i)
            return carry

        def attend_block(n, carry, head=head):
            i = plane_order(n)
            at = row_slab(i, outer_rows)
            mixed = jnp.dot(p_fresh[head, at, :], v_buf[head, 0], preferred_element_type=jnp.float32)
            mixed = mixed + jnp.dot(
                p_stale[head, at, :], v_buf[head, 1], preferred_element_type=jnp.float32
            )
            o_buf[head, at, :] = mixed.astype(jnp.bfloat16)

            @pl.when(jnp.logical_and(inner, i * LAYER == near_outer))
            def _():
                edge_part[head] = mixed

            @pl.when(jnp.logical_and(inner, i * LAYER == far_outer))
            def _():
                src = o_buf.at[head, row_slab(far_outer, tok_dev, LAYER), :]
                send(src, twin_part.at[head], sent, t_recv.at[head], twin)

            def give_back(j, carry):
                target = i * LAYER + j
                direct = jnp.logical_or(outer, is_inner(target, half))

                @pl.when(jnp.logical_and(target != me, direct))
                def _():
                    hand_out(head, target)

                return carry

            lax.fori_loop(0, LAYER, give_back, 0)
            return carry

        planes = devices // LAYER
        early = planes - HELD_BACK[head]
        lax.fori_loop(0, early, probs_block, 0)
        start_all(ISSUE[2 + 3 * head])
        arrived("V", head)
        start_all(ISSUE[3 + 3 * head])
        lax.fori_loop(0, early, attend_block, 0)
        if head > 0:
            join(head - 1)
        if early < planes:
            lax.fori_loop(early, planes, probs_block, 0)
            lax.fori_loop(early, planes, attend_block, 0)

    join(held - 1)
    for head in range(held):
        pltpu.make_async_copy(
            o_buf.at[head, row_slab(me, tok_dev), :],
            parts_ref.at[side, :, columns(head * half + my_group)],
            o_recv.at[head],
        ).start()
        pltpu.make_async_copy(
            lse.at[head, lax.div(me, owner_tile)], stats.at[head, me], s_recv.at[head]
        ).start()

    def outputs_in(head):
        @pl.when(inner)
        def _():
            whole_wait(o_buf.at[head], o_recv.at[head])

        @pl.when(outer)
        def _():
            whole_wait(o_buf.at[head, 0 : (devices - LAYER) * tok_dev, :], o_recv.at[head])

    for head in range(held):
        whole_wait(stats.at[head], s_recv.at[head])

        def levels(of_side, head=head):
            return jnp.concatenate(
                [
                    stats[head, of_side * half + (group + of_side * LAYER) % half]
                    for group in range(half)
                ],
                axis=0,
            )

        share = 1.0 / (1.0 + jnp.exp(levels(1) - levels(0)))
        share = jnp.concatenate([share, jnp.zeros((128 - half, 128), jnp.float32)], axis=0)
        shares[...] = jnp.transpose(share)
        rows = row_slab(lax.rem(me, owner_tile), tok_dev)
        if head < held - 1:
            outputs_in(head)
            merge_slot(head, half, parts_ref, shares.at[rows, :], outer, side, parts_ref.at[0])
        else:
            shares_ref[...] = shares[rows, :]

    outputs_in(held - 1)
    whole_wait(stats.at[:, 0 : devices - 1], s_send)
    slab = tok_dev * HEAD_DIM

    def all_sent(slabs):
        whole_wait(p_fresh.at[:, 0 : slabs * slab // keys, :], sent)

    kv, out = 4 * (half - 1), devices - 1

    @pl.when(inner)
    def _():
        whole_wait(twin_lse, l_send)
        all_sent(kv + devices - 1 + LAYER + out)

    @pl.when(outer)
    def _():
        all_sent(kv + devices - 1 - LAYER + out)


def merge_slot(slot, half, parts, shares, outer, side, out):
    for head in range(slot * half, (slot + 1) * half):
        at = slice(head * HEAD_DIM, (head + 1) * HEAD_DIM)

        def both(at=at, head=head):
            low, high = parts[0, :, at].astype(jnp.float32), parts[1, :, at].astype(jnp.float32)
            share = shares[:, head % half : head % half + 1]
            out[:, at] = (high + (low - high) * share).astype(jnp.bfloat16)

        if head % half < LAYER:
            both()
        else:
            pl.when(jnp.logical_not(outer))(both)

            @pl.when(outer)
            def _(at=at):
                out[:, at] = parts[side, :, at]


def merge_kernel(devices, parts, shares, out_ref, merged, out_sems):
    half = devices // 2
    me = lax.axis_index("tok")
    side = lax.div(me, half)
    inner = is_inner(me, half)
    outer = jnp.logical_not(inner)
    last = HEADS // half - 1
    middle = last * half + LAYER
    done, joined = last * half * HEAD_DIM, middle * HEAD_DIM

    def put(source, n, begin, end):
        return pltpu.make_async_copy(
            source.at[:, begin:end], out_ref.at[:, begin:end], out_sems.at[n]
        )

    put(parts.at[0], 0, 0, done).start()

    @pl.when(outer)
    def _():
        put(parts.at[side], 2, joined, HEADS * HEAD_DIM).start()

    def merge(heads):
        for head in heads:
            at = slice(head * HEAD_DIM, (head + 1) * HEAD_DIM)
            low, high = parts[0, :, at].astype(jnp.float32), parts[1, :, at].astype(jnp.float32)
            share = shares[:, head % half : head % half + 1]
            merged[:, at] = (high + (low - high) * share).astype(jnp.bfloat16)

    merge(range(last * half, middle))
    put(merged, 1, done, joined).start()

    @pl.when(inner)
    def _():
        merge(range(middle, HEADS))
        put(merged, 2, joined, HEADS * HEAD_DIM).start()

    put(parts.at[0], 0, 0, done).wait()
    put(merged, 1, done, joined).wait()
    put(merged, 2, joined, HEADS * HEAD_DIM).wait()


def halves(*arrays):
    arrays = [pltpu.with_memory_space_constraint(array, pltpu.HBM) for array in arrays]
    queries, fresh_keys, fresh_values, stale_keys, stale_values, patch_starts, order_starts = arrays
    devices = lax.axis_size("tok")
    tok_dev, width = queries.shape
    half = devices // 2
    held = HEADS // half
    tokens, keys = devices * tok_dev, half * tok_dev
    anywhere = pl.BlockSpec(memory_space=pl.ANY)
    main_memory = pl.BlockSpec(memory_space=pltpu.HBM)
    near_memory = pl.BlockSpec(memory_space=pltpu.VMEM)
    patches = patch_starts.shape[0]
    dma = pltpu.SemaphoreType.DMA
    parts, shares = pl.pallas_call(
        functools.partial(halves_kernel, devices),
        out_shape=(
            jax.ShapeDtypeStruct((2, tok_dev, width), jnp.bfloat16),
            jax.ShapeDtypeStruct((tok_dev, 128), jnp.float32),
        ),
        in_specs=[main_memory] * 7,
        out_specs=(near_memory, near_memory),
        scratch_shapes=[
            pltpu.VMEM((held, tokens, HEAD_DIM), jnp.bfloat16),
            pltpu.VMEM((held, 2, keys, HEAD_DIM), jnp.bfloat16),
            pltpu.VMEM((held, 2, keys, HEAD_DIM), jnp.bfloat16),
            pltpu.VMEM((held, tokens, keys), jnp.bfloat16),
            pltpu.VMEM((held, tokens, keys), jnp.bfloat16),
            pltpu.VMEM((held, tokens, HEAD_DIM), jnp.bfloat16),
            pltpu.VMEM((held, devices, 1, 128), jnp.float32),
            pltpu.VMEM((128, 128), jnp.float32),
            pltpu.VMEM((tokens, HEAD_DIM), jnp.int32),
            pltpu.VMEM((8, keys), jnp.int32),
            dma,
            dma((held, devices // LAYER)),
            dma((held,)),
            dma((held,)),
            dma((held,)),
            dma,
            dma((held,)),
            pltpu.SemaphoreType.REGULAR,
            pltpu.SemaphoreType.REGULAR,
            pltpu.SMEM((2, patches), jnp.int32),
            dma((2,)),
            pltpu.VMEM((held, tokens // 128, 1, 128), jnp.float32),
            pltpu.VMEM((held, LAYER * tok_dev // 128, 1, 128), jnp.float32),
            pltpu.VMEM((held, LAYER * tok_dev, HEAD_DIM), jnp.bfloat16),
            pltpu.VMEM((held, LAYER * tok_dev, HEAD_DIM), jnp.float32),
            dma,
            dma((held,)),
            dma((held,)),
        ],
        compiler_params=pltpu.CompilerParams(
            collective_id=0, has_side_effects=True, vmem_limit_bytes=32 * 1024 * 1024
        ),
    )(patch_starts, order_starts, queries, fresh_keys, stale_keys, fresh_values, stale_values)
    return pl.pallas_call(
        functools.partial(merge_kernel, devices),
        out_shape=jax.ShapeDtypeStruct((tok_dev, width), jnp.bfloat16),
        in_specs=[near_memory, near_memory],
        out_specs=main_memory,
        scratch_shapes=[pltpu.VMEM((tok_dev, width), jnp.bfloat16), dma((3,))],
        compiler_params=pltpu.CompilerParams(vmem_limit_bytes=16 * 1024 * 1024),
    )(parts, shares)


def solution(mesh):
    placed = (P(("groups", "tok"), None),) * 5 + (P("groups"),) * 2
    devices = mesh.shape["tok"]

    def body(*arrays):
        tok_dev = arrays[0].shape[0]
        split = devices % 2 == 0 and HEADS % (devices // 2) == 0
        split = split and devices // 2 == 2 * LAYER and LAYER * tok_dev % 128 == 0
        split = split and 2 * LAYER * tok_dev == 512
        split = split and 128 % tok_dev == 0 and devices * tok_dev % 512 == 0
        return (halves if split else shards)(*arrays)

    return jax.shard_map(
        body, mesh=mesh, in_specs=placed, out_specs=P(("groups", "tok"), None), check_vma=False
    )
```

```python
import functools
import math

import jax
import jax.numpy as jnp
from jax import lax
from jax.experimental import pallas as pl
from jax.experimental.pallas import tpu as pltpu
from jax.sharding import PartitionSpec as P

HEADS = 16
HEAD_DIM = 128
LAYER = 4
ISSUE = ((('Q', 0, ('straight',), None), ('K', 0, ('straight',), None), ('Q', 0, ('beside',), None), ('wide', 0, (), None), ('Q', 0, ('diagonal',), None), ('K', 0, ('diagonal',), None), ('K', 0, ('beside',), None), ('ready', 0, (), None), ('Q', 0, ('far',), None), ('V', 0, ('straight', 'beside', 'diagonal'), None), ('Q', 1, ('straight', 'diagonal'), 'outer'), ('Q', 1, ('beside',), None), ('pass', 0, (), None), ('Q', 1, ('far',), None), ('K', 1, ('straight', 'beside', 'diagonal'), None), ('V', 1, ('straight', 'beside', 'diagonal'), None)), (), (('pass', 1, (), None), ('Q', 1, ('straight', 'diagonal'), 'inner')), (), (), (), ())
HELD_BACK = (0, 1)
MESH = pl.DeviceIdType.MESH


def attention_kernel(
    devices,
    patch_starts,
    order_starts,
    queries,
    fresh_keys,
    stale_keys,
    fresh_values,
    stale_values,
    out_ref,
    q_buf,
    kv_buf,
    p_fresh,
    p_stale,
    o_buf,
    q_rank,
    k_rank,
    send_sems,
    recv_sems,
    own_sem,
    out_send,
    out_recv,
):
    me = lax.axis_index("tok")
    tok_dev = queries.shape[0]
    group_size = devices // HEADS
    slab = tok_dev // group_size
    tokens = devices * tok_dev
    rows = devices * slab
    my_head = me // group_size
    my_member = me % group_size
    barrier = pltpu.get_barrier_semaphore()

    def peer_of(step):
        return lax.rem(me + step, devices)

    def columns(head):
        return pl.ds(pl.multiple_of(head * HEAD_DIM, HEAD_DIM), HEAD_DIM)

    def row_slab(index, size):
        return pl.ds(pl.multiple_of(index * size, size), size)

    def greet(step, carry):
        pl.semaphore_signal(barrier, inc=1, device_id={"tok": peer_of(step)}, device_id_type=MESH)
        return carry

    lax.fori_loop(1, devices, greet, 0)

    sources = (queries, fresh_keys, stale_keys, fresh_values, stale_values)

    def source_view(which, device):
        head, member = device // group_size, device % group_size
        if which == 0:
            return queries.at[row_slab(member, slab), columns(head)]
        return sources[which].at[:, columns(head)]

    def landing(which, device):
        if which == 0:
            return q_buf.at[row_slab(device, slab), :]
        return kv_buf.at[which - 1, row_slab(device, tok_dev), :]

    own = [
        pltpu.make_async_copy(source_view(which, me), landing(which, me), own_sem.at[which])
        for which in range(5)
    ]
    for copy in own:
        copy.start()
    pl.semaphore_wait(barrier, devices - 1)

    for which in range(5):

        def send(step, carry, which=which):
            peer = peer_of(step)
            pltpu.make_async_remote_copy(
                src_ref=source_view(which, peer),
                dst_ref=landing(which, me),
                send_sem=send_sems.at[which],
                recv_sem=recv_sems.at[which],
                device_id={"tok": peer},
                device_id_type=MESH,
            ).start()
            return carry

        lax.fori_loop(1, devices, send, 0)

    patches = patch_starts.shape[0]
    starts = [patch_starts[p] for p in range(patches)]
    orders = [order_starts[p] for p in range(patches)]
    ranks = []
    for p in range(patches):
        rank = jnp.int32(0)
        for i in range(patches):
            rank = rank + jnp.where(orders[i] == starts[p], jnp.int32(i), jnp.int32(0))
        ranks.append(rank)
    jumps = [ranks[0]] + [ranks[p] - ranks[p - 1] for p in range(1, patches)]

    def rank_at(positions):
        total = jnp.zeros(positions.shape, jnp.int32)
        for p in range(patches):
            total = total + jnp.where(positions >= starts[p], jumps[p], 0)
        return total

    k_rank[...] = rank_at(lax.broadcasted_iota(jnp.int32, k_rank.shape, 1))

    def fill_rank(device, carry):
        base = device * tok_dev + my_member * slab
        q_rank[row_slab(device, slab), :] = rank_at(
            base + lax.broadcasted_iota(jnp.int32, (slab, HEAD_DIM), 0)
        )
        return carry

    lax.fori_loop(0, devices, fill_rank, 0)

    def all_of(which):
        size = (devices - 1) * (slab if which == 0 else tok_dev)
        return q_buf.at[0:size, :] if which == 0 else kv_buf.at[which - 1, 0:size, :]

    def arrived(which):
        view = all_of(which)
        pltpu.make_async_copy(view, view, recv_sems.at[which]).wait()
        own[which].wait()

    for which in range(3):
        arrived(which)

    score_scale = 1.0 / math.sqrt(HEAD_DIM)
    block = max(slab, min(rows, (1 << 18) // tokens))
    blocks = rows // block
    dims = (((1,), (1,)), ((), ()))

    def probs_block(i, carry):
        at = row_slab(i, block)
        q = q_buf[at, :]
        fresh = lax.dot_general(q, kv_buf[0], dims, preferred_element_type=jnp.float32)
        stale = lax.dot_general(q, kv_buf[1], dims, preferred_element_type=jnp.float32)
        fresh_ok = k_rank[0:1, :] <= q_rank[at, 0:1]
        scores = jnp.where(fresh_ok, fresh, stale) * score_scale
        top = jnp.max(scores, axis=1, keepdims=True)
        weights = jnp.exp(scores - top)
        total = jnp.sum(weights, axis=1, keepdims=True)
        probs = weights * (1.0 / total)
        p_fresh[at, :] = jnp.where(fresh_ok, probs, 0.0).astype(jnp.bfloat16)
        p_stale[at, :] = jnp.where(fresh_ok, 0.0, probs).astype(jnp.bfloat16)
        return carry

    lax.fori_loop(0, blocks, probs_block, 0)

    for which in range(3, 5):
        arrived(which)

    per_block = block // slab

    def give_back(i):
        def one(j, carry):
            target = i * per_block + j

            @pl.when(target != me)
            def _():
                pltpu.make_async_remote_copy(
                    src_ref=o_buf.at[row_slab(target, slab), :],
                    dst_ref=out_ref.at[row_slab(my_member, slab), columns(my_head)],
                    send_sem=out_send,
                    recv_sem=out_recv,
                    device_id={"tok": target},
                    device_id_type=MESH,
                ).start()

            return carry

        lax.fori_loop(0, per_block, one, 0)

    def attend_block(i, carry):
        at = row_slab(i, block)
        mixed = jnp.dot(p_fresh[at, :], kv_buf[2], preferred_element_type=jnp.float32)
        mixed = mixed + jnp.dot(p_stale[at, :], kv_buf[3], preferred_element_type=jnp.float32)
        o_buf[at, :] = mixed.astype(jnp.bfloat16)
        give_back(i)
        return carry

    lax.fori_loop(0, blocks, attend_block, 0)
    mine = pltpu.make_async_copy(
        o_buf.at[row_slab(me, slab), :],
        out_ref.at[row_slab(my_member, slab), columns(my_head)],
        own_sem.at[0],
    )
    mine.start()
    for which in range(5):
        view = all_of(which)
        pltpu.make_async_copy(view, view, send_sems.at[which]).wait()
    view = o_buf.at[0 : (devices - 1) * slab, :]
    mine.wait()
    pltpu.make_async_copy(view, view, out_send).wait()
    pltpu.make_async_copy(view, view, out_recv).wait()


def shards(queries, fresh_keys, fresh_values, stale_keys, stale_values, patch_starts, order_starts):
    devices = lax.axis_size("tok")
    tok_dev, width = queries.shape
    slab = tok_dev // (devices // HEADS)
    tokens, rows = devices * tok_dev, devices * slab
    anywhere = pl.BlockSpec(memory_space=pl.ANY)
    scalars = pl.BlockSpec(memory_space=pltpu.SMEM)
    return pl.pallas_call(
        functools.partial(attention_kernel, devices),
        out_shape=jax.ShapeDtypeStruct((tok_dev, width), jnp.bfloat16),
        in_specs=[scalars] * 2 + [anywhere] * 5,
        out_specs=anywhere,
        scratch_shapes=[
            pltpu.VMEM((rows, HEAD_DIM), jnp.bfloat16),
            pltpu.VMEM((4, tokens, HEAD_DIM), jnp.bfloat16),
            pltpu.VMEM((rows, tokens), jnp.bfloat16),
            pltpu.VMEM((rows, tokens), jnp.bfloat16),
            pltpu.VMEM((rows, HEAD_DIM), jnp.bfloat16),
            pltpu.VMEM((rows, HEAD_DIM), jnp.int32),
            pltpu.VMEM((8, tokens), jnp.int32),
            pltpu.SemaphoreType.DMA((5,)),
            pltpu.SemaphoreType.DMA((5,)),
            pltpu.SemaphoreType.DMA((5,)),
            pltpu.SemaphoreType.DMA,
            pltpu.SemaphoreType.DMA,
        ],
        compiler_params=pltpu.CompilerParams(
            collective_id=0, has_side_effects=True, vmem_limit_bytes=60 * 1024 * 1024
        ),
    )(
        patch_starts,
        order_starts,
        queries,
        fresh_keys,
        stale_keys,
        fresh_values,
        stale_values,
    )


def rank_table(patch_starts, order_starts):
    patches = patch_starts.shape[0]
    starts = [patch_starts[p] for p in range(patches)]
    orders = [order_starts[p] for p in range(patches)]
    ranks = []
    for p in range(patches):
        rank = jnp.int32(0)
        for i in range(patches):
            rank = rank + jnp.where(orders[i] == starts[p], jnp.int32(i), jnp.int32(0))
        ranks.append(rank)
    jumps = [ranks[0]] + [ranks[p] - ranks[p - 1] for p in range(1, patches)]

    def rank_at(positions):
        total = jnp.zeros(positions.shape, jnp.int32)
        for p in range(patches):
            total = total + jnp.where(positions >= starts[p], jumps[p], 0)
        return total

    return rank_at


def seat(device, half):
    shift = jnp.where(device >= half, LAYER, 0)
    return lax.rem(lax.rem(device, half) + shift, half)


def is_inner(device, half):
    return seat(device, half) >= LAYER


def halves_kernel(
    devices,
    starts_in,
    orders_in,
    queries,
    fresh_keys,
    stale_keys,
    fresh_values,
    stale_values,
    parts_ref,
    shares_ref,
    q_buf,
    k_buf,
    v_buf,
    p_fresh,
    p_stale,
    o_buf,
    stats,
    shares,
    q_rank,
    k_rank,
    sent,
    q_recv,
    k_recv,
    v_recv,
    o_recv,
    s_send,
    s_recv,
    ready,
    wide,
    layout,
    layout_sem,
    lse,
    twin_lse,
    twin_part,
    edge_part,
    l_send,
    l_recv,
    t_recv,
):
    me = lax.axis_index("tok")
    tok_dev = queries.shape[0]
    half = devices // 2
    held = HEADS // half
    tokens = devices * tok_dev
    keys = half * tok_dev
    side, place = lax.div(me, half), lax.rem(me, half)
    outer_rows = LAYER * tok_dev
    my_group = seat(me, half)
    inner = my_group >= LAYER
    outer = jnp.logical_not(inner)
    plane = lax.div(me, LAYER)
    other_plane = plane + 1 - 2 * lax.rem(plane, 2)
    outward = jnp.where(side == 0, -LAYER, LAYER)
    twin = me - outward
    near_outer = jnp.where(side == 0, 0, devices - LAYER)
    far_outer = devices - LAYER - near_outer
    barrier = pltpu.get_barrier_semaphore()

    column = lax.rem(me, LAYER)
    mirror = me + 2 - LAYER * lax.div(column, 2)

    def straight_peer(step):
        return other_plane * LAYER + 2 * lax.div(column, 2) + step

    def diagonal_peer(step):
        return other_plane * LAYER + 2 - 2 * lax.div(column, 2) + step

    def far_peer(step):
        return (1 - side) * half + lax.rem(place + step, half)

    def columns(head):
        return pl.ds(pl.multiple_of(head * HEAD_DIM, HEAD_DIM), HEAD_DIM)

    def row_slab(index, size, count=1):
        return pl.ds(pl.multiple_of(index * size, size), size * count)

    def signal(sem, device):
        pl.semaphore_signal(sem, inc=1, device_id={"tok": device}, device_id_type=MESH)


    @pl.when(inner)
    def _():
        signal(barrier, twin)

    for step in range(1, LAYER):
        signal(barrier, plane * LAYER + lax.rem(me + step, LAYER))
    for step in range(2):
        signal(barrier, straight_peer(step))
    layout_copies = [
        pltpu.make_async_copy(whole, layout.at[n], layout_sem.at[n])
        for n, whole in enumerate((starts_in, orders_in))
    ]
    for copy in layout_copies:
        copy.start()

    def send(src, dst, send_sem, recv_sem, device):
        pltpu.make_async_remote_copy(
            src_ref=src,
            dst_ref=dst,
            send_sem=send_sem,
            recv_sem=recv_sem,
            device_id={"tok": device},
            device_id_type=MESH,
        ).start()

    sources = {"Q": (queries,), "K": (fresh_keys, stale_keys), "V": (fresh_values, stale_values)}
    def landed(kind, head):
        if kind == "Q":
            return q_recv.at[head, plane]
        return (k_recv if kind == "K" else v_recv).at[head]


    def landing(kind, head, which):
        if kind == "Q":
            return q_buf.at[head, row_slab(me, tok_dev), :]
        return (k_buf if kind == "K" else v_buf).at[head, which, row_slab(place, tok_dev), :]

    def source(kind, head, which, device):
        return sources[kind][which].at[:, columns(head * half + seat(device, half))]

    def share_out(kind, head, spread):
        def go(step, peer):
            for which in range(len(sources[kind])):
                send(
                    source(kind, head, which, peer),
                    landing(kind, head, which),
                    sent,
                    landed(kind, head),
                    peer,
                )

        def straight(step, carry):
            go(step, straight_peer(step))
            return carry

        def diagonal(step, carry):
            go(step, diagonal_peer(step))
            return carry

        def beside(step, carry):
            go(step, plane * LAYER + lax.rem(me + step, LAYER))
            return carry

        def far(step, carry):
            peer = far_peer(step)
            pl.when(jnp.logical_or(inner, jnp.logical_not(is_inner(peer, half))))(
                lambda: go(step, peer)
            )
            return carry

        if "straight" in spread:
            lax.fori_loop(0, 2, straight, 0)
        if "beside" in spread:
            lax.fori_loop(1, LAYER, beside, 0)
        if "diagonal" in spread:
            lax.fori_loop(0, 2, diagonal, 0)
        if "far" in spread:
            lax.fori_loop(0, half, far, 0)

    def pass_on(head):
        @pl.when(inner)
        def _():
            view = q_buf.at[head, row_slab(near_outer, tok_dev, LAYER), :]
            pltpu.make_async_copy(view, view, q_recv.at[head, other_plane]).wait()
            send(view, view, sent, q_recv.at[head, other_plane], twin)

    def start_all(steps):
        for kind, head, spread, who in steps:
            if kind == "pass":
                pass_on(head)
            elif kind == "wide":
                pl.semaphore_wait(wide, 1)

                @pl.when(inner)
                def _():
                    signal(ready, twin)

            elif kind == "ready":
                pl.semaphore_wait(ready, 1)

                @pl.when(inner)
                def _():
                    signal(ready, me + outward)

            elif who is not None:
                pl.when(inner if who == "inner" else outer)(
                    lambda kind=kind, head=head, spread=spread: share_out(kind, head, spread)
                )
            else:
                share_out(kind, head, spread)

    pl.semaphore_wait(barrier, LAYER + 1 + inner.astype(jnp.int32))

    signal(wide, mirror)

    start_all(ISSUE[0])

    for head in range(held):
        for kind in "QKV":
            for which in range(len(sources[kind])):
                pltpu.make_async_copy(
                    source(kind, head, which, me), landing(kind, head, which), landed(kind, head)
                ).start()

    for copy in layout_copies:
        copy.wait()
    rank_at = rank_table(layout.at[0], layout.at[1])
    k_rank[...] = rank_at(keys * side + lax.broadcasted_iota(jnp.int32, k_rank.shape, 1))

    def fill_rank(device, carry):
        q_rank[row_slab(device, tok_dev), :] = rank_at(
            device * tok_dev + lax.broadcasted_iota(jnp.int32, (tok_dev, HEAD_DIM), 0)
        )
        return carry

    lax.fori_loop(0, devices, fill_rank, 0)

    def whole_wait(view, sem):
        pltpu.make_async_copy(view, view, sem).wait()

    def arrived(kind, head):
        whole_wait((k_buf if kind == "K" else v_buf).at[head], landed(kind, head))

    def asked(head, i):
        @pl.when(jnp.logical_not(jnp.logical_and(inner, i == other_plane)))
        def _():
            whole_wait(q_buf.at[head, row_slab(i, outer_rows), :], q_recv.at[head, i])

    score_scale = 1.0 / math.sqrt(HEAD_DIM)
    block = outer_rows
    dims = (((1,), (1,)), ((), ()))
    owner_tile = 128 // tok_dev
    edge_tiles = outer_rows // 128

    def plane_order(n):
        last = devices // LAYER - 1
        swapped = jnp.where(n >= 2, 5 - n, n)
        return jnp.where(side == 0, last - swapped, swapped)

    def send_levels(head, i):
        def one(j, carry):
            target = i * LAYER + j

            @pl.when(target != me)
            def _():
                src = lse.at[head, lax.div(target, owner_tile)]
                send(src, stats.at[head, me], s_send, s_recv.at[head], target)

            return carry

        lax.fori_loop(0, LAYER, one, 0)

        @pl.when(jnp.logical_and(inner, i * LAYER == far_outer))
        def _():
            src = lse.at[head, pl.ds(far_outer // owner_tile, edge_tiles)]
            send(src, twin_lse.at[head], l_send, l_recv.at[head], twin)

    def hand_out(head, target):
        send(
            o_buf.at[head, row_slab(target, tok_dev), :],
            parts_ref.at[side, :, columns(head * half + my_group)],
            sent,
            o_recv.at[head],
            target,
        )

    def join(head):
        @pl.when(inner)
        def _():
            whole_wait(twin_lse.at[head], l_recv.at[head])
            whole_wait(twin_part.at[head], t_recv.at[head])
            for tile in range(edge_tiles):
                mine, theirs = lse[head, near_outer // owner_tile + tile], twin_lse[head, tile]
                w_mine = jnp.broadcast_to(1.0 / (1.0 + jnp.exp(theirs - mine)), (128, 128))
                w_theirs = jnp.broadcast_to(1.0 / (1.0 + jnp.exp(mine - theirs)), (128, 128))
                spot = slice(tile * 128, (tile + 1) * 128)
                full = edge_part[head, spot, :] * jnp.transpose(w_mine)
                full = full + twin_part[head, spot, :].astype(jnp.float32) * jnp.transpose(w_theirs)
                at = pl.ds(pl.multiple_of(near_outer * tok_dev + tile * 128, 128), 128)
                o_buf[head, at, :] = full.astype(jnp.bfloat16)

            def one(j, carry):
                hand_out(head, near_outer + j)
                return carry

            lax.fori_loop(0, LAYER, one, 0)


    for head in range(held):
        arrived("K", head)
        start_all(ISSUE[1 + 3 * head])

        def probs_block(n, carry, head=head):
            i = plane_order(n)
            asked(head, i)
            at = row_slab(i, block)
            q = q_buf[head, at, :]
            fresh = lax.dot_general(q, k_buf[head, 0], dims, preferred_element_type=jnp.float32)
            stale = lax.dot_general(q, k_buf[head, 1], dims, preferred_element_type=jnp.float32)
            fresh_ok = k_rank[0:1, :] <= q_rank[at, 0:1]
            scores = jnp.where(fresh_ok, fresh, stale)
            top = jnp.max(scores, axis=1, keepdims=True)
            weights = jnp.exp2((scores - top) * (score_scale * math.log2(math.e)))
            total = jnp.sum(weights, axis=1, keepdims=True)
            probs = weights * (1.0 / total)
            p_fresh[head, at, :] = jnp.where(fresh_ok, probs, 0.0).astype(jnp.bfloat16)
            p_stale[head, at, :] = jnp.where(fresh_ok, 0.0, probs).astype(jnp.bfloat16)
            level = jnp.broadcast_to(top * score_scale + jnp.log(total), (block, 128))
            for tile in range(block // 128):
                turned = jnp.transpose(level[tile * 128 : (tile + 1) * 128, :])
                lse[head, i * (block // 128) + tile] = turned[0:1, :]
            send_levels(head, i)
            return carry

        def attend_block(n, carry, head=head):
            i = plane_order(n)
            at = row_slab(i, outer_rows)
            mixed = jnp.dot(p_fresh[head, at, :], v_buf[head, 0], preferred_element_type=jnp.float32)
            mixed = mixed + jnp.dot(
                p_stale[head, at, :], v_buf[head, 1], preferred_element_type=jnp.float32
            )
            o_buf[head, at, :] = mixed.astype(jnp.bfloat16)

            @pl.when(jnp.logical_and(inner, i * LAYER == near_outer))
            def _():
                edge_part[head] = mixed

            @pl.when(jnp.logical_and(inner, i * LAYER == far_outer))
            def _():
                src = o_buf.at[head, row_slab(far_outer, tok_dev, LAYER), :]
                send(src, twin_part.at[head], sent, t_recv.at[head], twin)

            def give_back(j, carry):
                target = i * LAYER + j
                direct = jnp.logical_or(outer, is_inner(target, half))

                @pl.when(jnp.logical_and(target != me, direct))
                def _():
                    hand_out(head, target)

                return carry

            lax.fori_loop(0, LAYER, give_back, 0)
            return carry

        planes = devices // LAYER
        early = planes - HELD_BACK[head]
        lax.fori_loop(0, early, probs_block, 0)
        start_all(ISSUE[2 + 3 * head])
        arrived("V", head)
        start_all(ISSUE[3 + 3 * head])
        lax.fori_loop(0, early, attend_block, 0)
        if head > 0:
            join(head - 1)
        if early < planes:
            lax.fori_loop(early, planes, probs_block, 0)
            lax.fori_loop(early, planes, attend_block, 0)

    join(held - 1)
    for head in range(held):
        pltpu.make_async_copy(
            o_buf.at[head, row_slab(me, tok_dev), :],
            parts_ref.at[side, :, columns(head * half + my_group)],
            o_recv.at[head],
        ).start()
        pltpu.make_async_copy(
            lse.at[head, lax.div(me, owner_tile)], stats.at[head, me], s_recv.at[head]
        ).start()

    def outputs_in(head):
        @pl.when(inner)
        def _():
            whole_wait(o_buf.at[head], o_recv.at[head])

        @pl.when(outer)
        def _():
            whole_wait(o_buf.at[head, 0 : (devices - LAYER) * tok_dev, :], o_recv.at[head])

    for head in range(held):
        whole_wait(stats.at[head], s_recv.at[head])

        def levels(of_side, head=head):
            return jnp.concatenate(
                [
                    stats[head, of_side * half + (group + of_side * LAYER) % half]
                    for group in range(half)
                ],
                axis=0,
            )

        share = 1.0 / (1.0 + jnp.exp(levels(1) - levels(0)))
        share = jnp.concatenate([share, jnp.zeros((128 - half, 128), jnp.float32)], axis=0)
        shares[...] = jnp.transpose(share)
        rows = row_slab(lax.rem(me, owner_tile), tok_dev)
        if head < held - 1:
            outputs_in(head)
            merge_slot(head, half, parts_ref, shares.at[rows, :], outer, side, parts_ref.at[0])
        else:
            shares_ref[...] = shares[rows, :]

    outputs_in(held - 1)
    whole_wait(stats.at[:, 0 : devices - 1], s_send)
    slab = tok_dev * HEAD_DIM

    def all_sent(slabs):
        whole_wait(p_fresh.at[:, 0 : slabs * slab // keys, :], sent)

    kv, out = 4 * (half - 1), devices - 1

    @pl.when(inner)
    def _():
        whole_wait(twin_lse, l_send)
        all_sent(kv + devices - 1 + LAYER + out)

    @pl.when(outer)
    def _():
        all_sent(kv + devices - 1 - LAYER + out)


def merge_slot(slot, half, parts, shares, outer, side, out):
    for head in range(slot * half, (slot + 1) * half):
        at = slice(head * HEAD_DIM, (head + 1) * HEAD_DIM)

        def both(at=at, head=head):
            low, high = parts[0, :, at].astype(jnp.float32), parts[1, :, at].astype(jnp.float32)
            share = shares[:, head % half : head % half + 1]
            out[:, at] = (high + (low - high) * share).astype(jnp.bfloat16)

        if head % half < LAYER:
            both()
        else:
            pl.when(jnp.logical_not(outer))(both)

            @pl.when(outer)
            def _(at=at):
                out[:, at] = parts[side, :, at]


def merge_kernel(devices, parts, shares, out_ref, merged, out_sems):
    half = devices // 2
    me = lax.axis_index("tok")
    side = lax.div(me, half)
    inner = is_inner(me, half)
    outer = jnp.logical_not(inner)
    last = HEADS // half - 1
    middle = last * half + LAYER
    done, joined = last * half * HEAD_DIM, middle * HEAD_DIM

    def put(source, n, begin, end):
        return pltpu.make_async_copy(
            source.at[:, begin:end], out_ref.at[:, begin:end], out_sems.at[n]
        )

    put(parts.at[0], 0, 0, done).start()

    @pl.when(outer)
    def _():
        put(parts.at[side], 2, joined, HEADS * HEAD_DIM).start()

    def merge(heads):
        for head in heads:
            at = slice(head * HEAD_DIM, (head + 1) * HEAD_DIM)
            low, high = parts[0, :, at].astype(jnp.float32), parts[1, :, at].astype(jnp.float32)
            share = shares[:, head % half : head % half + 1]
            merged[:, at] = (high + (low - high) * share).astype(jnp.bfloat16)

    merge(range(last * half, middle))
    put(merged, 1, done, joined).start()

    @pl.when(inner)
    def _():
        merge(range(middle, HEADS))
        put(merged, 2, joined, HEADS * HEAD_DIM).start()

    put(parts.at[0], 0, 0, done).wait()
    put(merged, 1, done, joined).wait()
    put(merged, 2, joined, HEADS * HEAD_DIM).wait()


def halves(*arrays):
    arrays = [pltpu.with_memory_space_constraint(array, pltpu.HBM) for array in arrays]
    queries, fresh_keys, fresh_values, stale_keys, stale_values, patch_starts, order_starts = arrays
    devices = lax.axis_size("tok")
    tok_dev, width = queries.shape
    half = devices // 2
    held = HEADS // half
    tokens, keys = devices * tok_dev, half * tok_dev
    anywhere = pl.BlockSpec(memory_space=pl.ANY)
    main_memory = pl.BlockSpec(memory_space=pltpu.HBM)
    near_memory = pl.BlockSpec(memory_space=pltpu.VMEM)
    patches = patch_starts.shape[0]
    dma = pltpu.SemaphoreType.DMA
    parts, shares = pl.pallas_call(
        functools.partial(halves_kernel, devices),
        out_shape=(
            jax.ShapeDtypeStruct((2, tok_dev, width), jnp.bfloat16),
            jax.ShapeDtypeStruct((tok_dev, 128), jnp.float32),
        ),
        in_specs=[main_memory] * 7,
        out_specs=(near_memory, near_memory),
        scratch_shapes=[
            pltpu.VMEM((held, tokens, HEAD_DIM), jnp.bfloat16),
            pltpu.VMEM((held, 2, keys, HEAD_DIM), jnp.bfloat16),
            pltpu.VMEM((held, 2, keys, HEAD_DIM), jnp.bfloat16),
            pltpu.VMEM((held, tokens, keys), jnp.bfloat16),
            pltpu.VMEM((held, tokens, keys), jnp.bfloat16),
            pltpu.VMEM((held, tokens, HEAD_DIM), jnp.bfloat16),
            pltpu.VMEM((held, devices, 1, 128), jnp.float32),
            pltpu.VMEM((128, 128), jnp.float32),
            pltpu.VMEM((tokens, HEAD_DIM), jnp.int32),
            pltpu.VMEM((8, keys), jnp.int32),
            dma,
            dma((held, devices // LAYER)),
            dma((held,)),
            dma((held,)),
            dma((held,)),
            dma,
            dma((held,)),
            pltpu.SemaphoreType.REGULAR,
            pltpu.SemaphoreType.REGULAR,
            pltpu.SMEM((2, patches), jnp.int32),
            dma((2,)),
            pltpu.VMEM((held, tokens // 128, 1, 128), jnp.float32),
            pltpu.VMEM((held, LAYER * tok_dev // 128, 1, 128), jnp.float32),
            pltpu.VMEM((held, LAYER * tok_dev, HEAD_DIM), jnp.bfloat16),
            pltpu.VMEM((held, LAYER * tok_dev, HEAD_DIM), jnp.float32),
            dma,
            dma((held,)),
            dma((held,)),
        ],
        compiler_params=pltpu.CompilerParams(
            collective_id=0, has_side_effects=True, vmem_limit_bytes=32 * 1024 * 1024
        ),
    )(patch_starts, order_starts, queries, fresh_keys, stale_keys, fresh_values, stale_values)
    return pl.pallas_call(
        functools.partial(merge_kernel, devices),
        out_shape=jax.ShapeDtypeStruct((tok_dev, width), jnp.bfloat16),
        in_specs=[near_memory, near_memory],
        out_specs=main_memory,
        scratch_shapes=[pltpu.VMEM((tok_dev, width), jnp.bfloat16), dma((3,))],
        compiler_params=pltpu.CompilerParams(vmem_limit_bytes=16 * 1024 * 1024),
    )(parts, shares)


def solution(mesh):
    placed = (P(("groups", "tok"), None),) * 5 + (P("groups"),) * 2
    devices = mesh.shape["tok"]

    def body(*arrays):
        tok_dev = arrays[0].shape[0]
        split = devices % 2 == 0 and HEADS % (devices // 2) == 0
        split = split and devices // 2 == 2 * LAYER and LAYER * tok_dev % 128 == 0
        split = split and 2 * LAYER * tok_dev == 512
        split = split and 128 % tok_dev == 0 and devices * tok_dev % 512 == 0
        return (halves if split else shards)(*arrays)

    return jax.shard_map(
        body, mesh=mesh, in_specs=placed, out_specs=P(("groups", "tok"), None), check_vma=False
    )
```
